32 devices in a mesh: blk: 4 (over y, x), grid: 8 (over z, core).
Axes of the slice: x: 2, y: 2, z: 4, core: 2. Of those that a mesh axis runs over, the one named last changes fastest.
Arguments:
- conn: int32 [2048, 9], P(('blk', 'grid')), may hold values from 0 to 2047, as said below
- extract: float32 [9, 9, 2048], P(None, None, ('blk', 'grid')), may hold values from 0.1 to 1
- points: float32 [3, 9, 2048], P(None, None, ('blk', 'grid')), as said below
Outputs:
- factor: float32 [2, 1024, 4, 512], P(None, 'grid', None, 'blk')
The draws below stay inside these ranges and needn't reach their ends.
Inputs may be any that keep to these rules, and one draw needn't show every extreme that they name: `conn`: element e = ix 32 + iy of the periodic 64 x 32 grid of elements names the functions ((ix + s) mod 64) * 32 + (iy + t) mod 32 for s, t in 0, 1, 2, each once, in an order that differs from element to element. The 9 points of element e = ix 32 + iy are the 3 x 3 Gauss points of the cell [ix / 64, (ix + 1) / 64] x [iy / 64, (iy + 1) / 64], each coordinate then moved by at most 3.5 / 64; points[2] is positive.
All inputs are finite; a program needn't handle non-finite values.
Results may differ from the reference program's by a relative error of at most 0.0003.
Values sent between devices are 32-bit elements; how exact they have to be, the bound alone decides.
No kernel may reach another device: no remote copies, remote signals or barrier semaphores. Data moves between devices by JAX's collectives and lax.ppermute only.
A program may use at most 128 MiB of HBM per device.

```python
import math
import jax
import jax.numpy as jnp
from jax import lax

M = 2048
EX = 64
EY = 32
E = 2048
QP = 9
TB = 128
RCY = 2
CCY = 4
N_BLK = 4
N_GRID = 8


def draw_points(key, part):
    phase_key, amp_key, weight_key, jitter_key = jax.random.split(key, 4)
    phases = jax.random.uniform(phase_key, (3,), jnp.float32, 0.0, 2.0 * math.pi)
    amplitude = jax.random.uniform(amp_key, (2,), jnp.float32, 0.25, 1.0) / EX
    jitter = jax.random.uniform(jitter_key, (2, QP, E), jnp.float32, -2.5, 2.5) / EX
    height = EY / EX
    spread_root = 0.5 * math.sqrt(0.6)
    gauss_nodes = jnp.array([0.5 - spread_root, 0.5, 0.5 + spread_root], jnp.float32)
    element = jnp.arange(E, dtype=jnp.int32)
    cell_x = (element // EY).astype(jnp.float32)
    cell_y = (element % EY).astype(jnp.float32)
    local_x = jnp.repeat(gauss_nodes, 3)
    local_y = jnp.tile(gauss_nodes, 3)
    base_x = (cell_x[None, :] + local_x[:, None]) / EX
    base_y = (cell_y[None, :] + local_y[:, None]) / EX
    place_x = base_x + amplitude[0] * jnp.sin(2.0 * math.pi * base_y / height + phases[0]) + jitter[0]
    place_y = base_y + amplitude[1] * jnp.sin(2.0 * math.pi * base_x + phases[1]) + jitter[1]
    weight = jnp.exp(jax.random.uniform(weight_key, (QP, E), jnp.float32, math.log(0.05), math.log(0.5)))
    return jnp.stack([place_x, place_y, weight], axis=0)


def draw_conn(key, part):
    turn = jax.random.randint(key, (E,), 0, 8)
    element = jnp.arange(E, dtype=jnp.int32)
    cell_x = element // EY
    cell_y = element % EY
    local = jnp.arange(QP, dtype=jnp.int32)
    first_step = local // 3
    second_step = local % 3
    swapped = (turn // 4)[:, None] == 1
    step_x = jnp.where(swapped, second_step[None, :], first_step[None, :])
    step_y = jnp.where(swapped, first_step[None, :], second_step[None, :])
    step_x = jnp.where((turn % 2)[:, None] == 1, 2 - step_x, step_x)
    step_y = jnp.where((turn // 2 % 2)[:, None] == 1, 2 - step_y, step_y)
    return (cell_x[:, None] + step_x) % EX * EY + (cell_y[:, None] + step_y) % EY


def block_levels(own_key, dims, pieces, smallest, high):
    loudness, own = 1.0, jax.random.fold_in(own_key, 6)
    for axis_at, blocks in pieces:
        draws = jnp.exp(jax.random.uniform(jax.random.fold_in(own, axis_at), (blocks,), jnp.float32, smallest / len(pieces), high / len(pieces)))
        loudness = loudness * jnp.repeat(draws, dims[axis_at] // blocks).reshape([-1 if axis == axis_at else 1 for axis in range(len(dims))])
    return loudness


def setup_inputs(seed: int = 0) -> dict:
    key_of = jax.random.split(jax.random.key(seed), 4)
    return {
        "conn": draw_conn(jax.random.fold_in(key_of[3], 71), 0),
        "extract": jnp.clip(0.1 + 0.9 * jax.random.uniform(key_of[1], (QP, QP, E), jnp.float32) ** block_levels(key_of[1], (QP, QP, E), ((2, 32),), -0.2, 0.2), 0.1, 1.0),
        "points": draw_points(jax.random.fold_in(key_of[3], 71), 0),
    }


kernel_gain = 0.02
mass_shift = 0.05

def bernstein_table():
    spread_root = 0.5 * math.sqrt(0.6)
    gauss_nodes = [0.5 - spread_root, 0.5, 0.5 + spread_root]

    def bern_poly(which, where):
        return [(1.0 - where) ** 2, 2.0 * where * (1.0 - where), where * where][which]
    table_rows = []
    for i in range(3):
        for j in range(3):
            table_row = []
            for a in range(3):
                for b in range(3):
                    table_row.append(bern_poly(a, gauss_nodes[i]) * bern_poly(b, gauss_nodes[j]))
            table_rows.append(table_row)
    return jnp.asarray(table_rows, jnp.float32)

def torus_square(first_x, first_y, second_x, second_y):
    height = EY / EX
    gap_x = jnp.abs(first_x - second_x)
    gap_x = jnp.minimum(gap_x, jnp.abs(1.0 - gap_x))
    gap_y = jnp.abs(first_y - second_y)
    gap_y = jnp.minimum(gap_y, jnp.abs(height - gap_y))
    return gap_x * gap_x + gap_y * gap_y

def kernel_rows(test_x, test_y, trial_x, trial_y, trial_w):
    distance = torus_square(test_x[:, None], test_y[:, None], trial_x[None, :], trial_y[None, :])
    return kernel_gain * trial_w[None, :] * (1.0 + distance * (EX * EX / 4.0)) ** (-1.75)

def reference(conn, extract, points):
    values = jnp.einsum('kb,abe->eka', bernstein_table(), extract, precision=lax.Precision.HIGHEST)
    place_x = points[0].T.reshape(-1)
    place_y = points[1].T.reshape(-1)
    weight = points[2].T.reshape(-1)
    flat_conn = conn.reshape(-1)
    span = math.gcd(E, 128)
    rows = span * QP
    slot = jnp.arange(rows, dtype=jnp.int32).reshape(span, QP)
    row_index = jnp.broadcast_to(slot[:, :, None], (span, QP, QP))

    def one_block(stiff, index):
        start = (index * span).astype(jnp.int32)
        block_x = lax.dynamic_slice_in_dim(place_x, start * QP, rows)
        block_y = lax.dynamic_slice_in_dim(place_y, start * QP, rows)
        block_w = lax.dynamic_slice_in_dim(weight, start * QP, rows)
        block_vals = lax.dynamic_slice_in_dim(values, start, span, 0)
        block_conn = lax.dynamic_slice_in_dim(conn, start, span, 0)
        kernel_block = kernel_rows(block_x, block_y, place_x, place_y, weight)
        total = lax.optimization_barrier(jnp.sum(kernel_block, axis=1))
        summed = jnp.einsum('pek,eka->pea', kernel_block.reshape(rows, E, QP), values, precision=lax.Precision.HIGHEST)
        potential = jnp.zeros((rows, M), jnp.float32).at[:, flat_conn].add(summed.reshape(rows, E * QP))
        col_index = jnp.broadcast_to(block_conn[:, None, :], (span, QP, QP))
        phi_rows = jnp.zeros((rows, M), jnp.float32).at[row_index, col_index].add(block_vals)
        share = block_w[:, None] * ((mass_shift + total)[:, None] * phi_rows - potential)
        contrib = jnp.einsum('eka,ekm->eam', block_vals, share.reshape(span, QP, M), precision=lax.Precision.HIGHEST)
        stiff = stiff.at[block_conn.reshape(-1)].add(contrib.reshape(span * QP, M))
        return (stiff, None)
    stiff, unused = lax.scan(one_block, jnp.zeros((M, M), jnp.float32), jnp.arange(E // span, dtype=jnp.int32))
    head = stiff[:TB, :TB]
    lower = jnp.linalg.cholesky(0.5 * (head + head.T))
    rest = lax.linalg.triangular_solve(lower, stiff[TB:, :TB], left_side=False, lower=True, transpose_a=True)
    trail = stiff[TB:, TB:] - jnp.dot(rest.astype(jnp.float32), rest.T.astype(jnp.float32), precision=lax.Precision.HIGHEST, preferred_element_type=jnp.float32)
    top_rows = jnp.concatenate([lower, jnp.zeros((TB, M - TB), jnp.float32)], axis=1)
    bottom_rows = jnp.concatenate([rest, trail], axis=1)
    whole = jnp.tril(jnp.concatenate([top_rows, bottom_rows], axis=0))
    return whole.reshape(RCY, N_GRID * TB, CCY, N_BLK * TB)
```

```python
import functools
import math

import jax
import jax.numpy as jnp
from jax import lax
from jax.experimental import pallas as pl
from jax.experimental.pallas import tpu as pltpu
from jax.sharding import PartitionSpec as P

M = 2048
EX = 64
EY = 32
QP = 9
TB = 128

KERNEL_GAIN = 0.02
MASS_SHIFT = 0.05

TILE_IX = TB // EY
WIN_IX = TILE_IX + 2
WIN = WIN_IX * EY
HALO = WIN - TB
COLS = 256
POINTS = QP * TB
GROUPS = 3 + QP
KROWS = 16
SUB = 3
HALF = EX / 2.0
ROUND_X = 1.5 * 2.0**23 * HALF
ROUND_Y = 1.5 * 2.0**23 * (HALF * EY / EX)


def bernstein_table():
    spread_root = 0.5 * math.sqrt(0.6)
    gauss_nodes = [0.5 - spread_root, 0.5, 0.5 + spread_root]

    def bern_poly(which, where):
        return [(1.0 - where) ** 2, 2.0 * where * (1.0 - where), where * where][which]

    table_rows = []
    for i in range(3):
        for j in range(3):
            table_row = []
            for a in range(3):
                for b in range(3):
                    table_row.append(bern_poly(a, gauss_nodes[i]) * bern_poly(b, gauss_nodes[j]))
            table_rows.append(table_row)
    return jnp.asarray(table_rows, jnp.float32)


def ring(size, shift):
    return [(i, (i + shift) % size) for i in range(size)]


def gather_axis(x, axis):
    size = lax.axis_size(axis)
    at = lax.axis_index(axis)
    got = [x] + [lax.ppermute(x, axis, ring(size, s)) for s in range(1, size)]
    back = jnp.stack(got[::-1] + got[::-1])
    return lax.dynamic_slice_in_dim(back, size - 1 - at, size, 0)


def local_pack(conn, extract, points, first):
    count = conn.shape[0]
    element = first + jnp.arange(count, dtype=jnp.int32)
    step_x = (conn // EY - (element // EY)[:, None]) % EX
    step_y = (conn % EY - (element % EY)[:, None]) % EY
    slot = (3 * step_x + step_y).T
    values = jnp.einsum("kb,abn->akn", bernstein_table(), extract, precision=lax.Precision.HIGHEST)
    names = jnp.arange(QP, dtype=jnp.int32)
    ordered = jnp.sum(
        jnp.where(slot[None, :, None, :] == names[:, None, None, None], values[None], 0.0), axis=1
    )
    scaled = jnp.concatenate([points[:2] * HALF, points[2:]], axis=0)
    return jnp.concatenate([scaled, ordered], axis=0)


def store_basis(data, tile, scale, hi_ref, lo_ref):
    lane = lax.broadcasted_iota(jnp.int32, (1, TB), 1)
    column = lane // EY
    fy = lax.broadcasted_iota(jnp.int32, (EY, TB), 0)
    iy = lax.broadcasted_iota(jnp.int32, (EY, TB), 1) % EY
    step = (fy - iy + EY) % EY
    masks = [step == t for t in range(3)]
    for fx in range(WIN_IX):
        hi, lo = [], []
        for t in range(3):
            rows = jnp.zeros((KROWS, TB), jnp.float32)
            for ix in range(TILE_IX):
                if 0 <= fx - ix < 3:
                    rows = jnp.where(column == ix, data[tile, 3 + 3 * (fx - ix) + t], rows)
            rows = rows * scale
            top = rows.astype(jnp.bfloat16).astype(jnp.float32)
            hi.append(top)
            lo.append(rows - top)
        for k in range(QP):
            for parts, ref in ((hi, hi_ref), (lo, lo_ref)):
                block = jnp.zeros((EY, TB), jnp.float32)
                for t in range(3):
                    block = jnp.where(masks[t], parts[t][k : k + 1], block)
                ref[fx * EY : (fx + 1) * EY, k * TB : (k + 1) * TB] = block.astype(jnp.bfloat16)


def store_weight(data, tile, hi_ref, lo_ref):
    first = lax.broadcasted_iota(jnp.int32, (COLS - WIN, TB), 0) == 0
    rows = data[tile, 2]
    top = rows.astype(jnp.bfloat16).astype(jnp.float32)
    for k in range(QP):
        for part, ref in ((top, hi_ref), (rows - top, lo_ref)):
            block = jnp.where(first, part[k : k + 1], 0.0)
            ref[WIN:, k * TB : (k + 1) * TB] = block.astype(jnp.bfloat16)


def nt(a, b):
    return lax.dot_general(a, b, (((1,), (1,)), ((), ())), preferred_element_type=jnp.float32)


def nn(a, b):
    return lax.dot_general(a, b, (((1,), (0,)), ((), ())), preferred_element_type=jnp.float32)


def kernel_block(xp, yp, xq, yq):
    gx = xp - xq
    gx = gx - ((gx + ROUND_X) - ROUND_X)
    gy = yp - yq
    gy = gy - ((gy + ROUND_Y) - ROUND_Y)
    inverse = lax.rsqrt(gx * gx + gy * gy + 1.0)
    square = inverse * inverse
    return square * square * lax.rsqrt(inverse)


def tile_body(
    tile_cols, rows_ref, cols_ref, data, main_ref, halo_ref, total_ref,
    xp_ref, yp_ref, rhi, rlo, chi, clo, ghi, glo, pot,
):
    r = pl.program_id(0)
    c = pl.program_id(1)
    row_tile = rows_ref[r]
    col_tile = cols_ref[c]

    @pl.when(c == 0)
    def _():
        store_basis(data, row_tile, data[row_tile, 2], rhi, rlo)
        for k in range(QP):
            for group, ref in ((0, xp_ref), (1, yp_ref)):
                row = jnp.broadcast_to(data[row_tile, group, k : k + 1, :], (TB, TB))
                ref[k * TB : (k + 1) * TB, :] = row.T
        total_ref[...] = jnp.zeros_like(total_ref)

    store_basis(data, col_tile, data[col_tile, 2], chi, clo)
    store_weight(data, col_tile, chi, clo)
    step_rows = 32
    blocks = QP // SUB

    def evaluate(block):
        slot = block % 2
        for i in range(SUB * TB // step_rows):
            at = block * SUB * TB + i * step_rows
            xp = xp_ref[at : at + step_rows, :]
            yp = yp_ref[at : at + step_rows, :]
            for k in range(QP):
                g = kernel_block(
                    xp, yp, data[col_tile, 0, k : k + 1, :], data[col_tile, 1, k : k + 1, :]
                )
                top = g.astype(jnp.bfloat16)
                where = (slot, slice(i * step_rows, (i + 1) * step_rows), slice(k * TB, (k + 1) * TB))
                ghi[where] = top
                glo[where] = (g - top.astype(jnp.float32)).astype(jnp.bfloat16)

    def contract(block):
        slot = block % 2
        part = nt(ghi[slot], chi[...]) + nt(ghi[slot], clo[...]) + nt(glo[slot], chi[...])
        pot[block * SUB * TB : (block + 1) * SUB * TB, :] = part

    for block in range(blocks):
        evaluate(block)
        if block:
            contract(block - 1)
    contract(blocks - 1)

    for k in range(QP):
        turned = pot[k * TB : (k + 1) * TB, TB:].T
        total_ref[0, k : k + 1, :] += KERNEL_GAIN * turned[HALO : HALO + 1, :]
    full = pot[...]
    top = full.astype(jnp.bfloat16)
    rest = (full - top.astype(jnp.float32)).astype(jnp.bfloat16)
    stiff = -KERNEL_GAIN * (nn(rhi[...], top) + nn(rlo[...], top) + nn(rhi[...], rest))
    main_ref[0, 0] = stiff[:, :TB]

    @pl.when(c % 2 == 0)
    def _():
        halo_ref[0, 0, :, :HALO] = stiff[:, TB:WIN]

    @pl.when(c % 2 == 1)
    def _():
        halo_ref[0, 0, :, HALO:] = stiff[:, TB:WIN]


def stiffness_tiles(row_tiles, col_tiles, data):
    tile_rows, tile_cols = row_tiles.shape[0], col_tiles.shape[0]
    f32, b16 = jnp.float32, jnp.bfloat16
    return pl.pallas_call(
        functools.partial(tile_body, tile_cols),
        out_shape=(
            jax.ShapeDtypeStruct((tile_rows, tile_cols, WIN, TB), f32),
            jax.ShapeDtypeStruct((tile_rows, tile_cols // 2, WIN, TB), f32),
            jax.ShapeDtypeStruct((tile_rows, KROWS, TB), f32),
        ),
        grid_spec=pltpu.PrefetchScalarGridSpec(
            num_scalar_prefetch=2,
            grid=(tile_rows, tile_cols),
            in_specs=[pl.BlockSpec(data.shape, lambda r, c, *_: (0, 0, 0, 0))],
            out_specs=(
                pl.BlockSpec((1, 1, WIN, TB), lambda r, c, *_: (r, c, 0, 0)),
                pl.BlockSpec((1, 1, WIN, TB), lambda r, c, *_: (r, c // 2, 0, 0)),
                pl.BlockSpec((1, KROWS, TB), lambda r, c, *_: (r, 0, 0)),
            ),
            scratch_shapes=[
                pltpu.VMEM((POINTS, TB), f32),
                pltpu.VMEM((POINTS, TB), f32),
                pltpu.VMEM((WIN, POINTS), b16),
                pltpu.VMEM((WIN, POINTS), b16),
                pltpu.VMEM((COLS, POINTS), b16),
                pltpu.VMEM((COLS, POINTS), b16),
                pltpu.VMEM((2, SUB * TB, POINTS), b16),
                pltpu.VMEM((2, SUB * TB, POINTS), b16),
                pltpu.VMEM((POINTS, COLS), f32),
            ],
        ),
        compiler_params=pltpu.CompilerParams(dimension_semantics=("arbitrary", "arbitrary")),
    )(row_tiles, col_tiles, data)


def mass_body(rows_ref, data, total_ref, mass_ref, lhi, llo, bhi, blo):
    r = pl.program_id(0)
    row_tile = rows_ref[r]
    scale = data[row_tile, 2] * (MASS_SHIFT + total_ref[0])
    store_basis(data, row_tile, scale, lhi, llo)
    store_basis(data, row_tile, jnp.ones((KROWS, TB), jnp.float32), bhi, blo)
    mass_ref[0] = nt(lhi[...], bhi[...]) + nt(llo[...], bhi[...]) + nt(lhi[...], blo[...])


def mass_windows(row_tiles, data, total):
    tile_rows = row_tiles.shape[0]
    return pl.pallas_call(
        mass_body,
        out_shape=jax.ShapeDtypeStruct((tile_rows, WIN, WIN), jnp.float32),
        grid_spec=pltpu.PrefetchScalarGridSpec(
            num_scalar_prefetch=1,
            grid=(tile_rows,),
            in_specs=[
                pl.BlockSpec(data.shape, lambda r, *_: (0, 0, 0, 0)),
                pl.BlockSpec((1, KROWS, TB), lambda r, *_: (r, 0, 0)),
            ],
            out_specs=pl.BlockSpec((1, WIN, WIN), lambda r, *_: (r, 0, 0)),
            scratch_shapes=[pltpu.VMEM((WIN, POINTS), jnp.bfloat16)] * 4,
        ),
        compiler_params=pltpu.CompilerParams(dimension_semantics=("arbitrary",)),
    )(row_tiles, data, total)


def shards(conn, extract, points):
    count = conn.shape[0]
    grid_size = lax.axis_size("grid")
    blk_size = lax.axis_size("blk")
    grid_at = lax.axis_index("grid")
    blk_at = lax.axis_index("blk")
    tiles = M // TB
    tile_rows = tiles // grid_size
    tile_cols = tiles // blk_size

    own = local_pack(conn, extract, points, (blk_at * grid_size + grid_at) * count)
    own = own.reshape(-1)
    every = gather_axis(gather_axis(own, "blk"), "grid")
    every = every.transpose(1, 0, 2).reshape(tiles, TB // count, GROUPS, QP, count)
    data = every.transpose(0, 2, 3, 1, 4).reshape(tiles, GROUPS, QP, TB)
    data = jnp.pad(data, ((0, 0), (0, 0), (0, KROWS - QP), (0, 0)))

    row_tiles = jnp.arange(tile_rows, dtype=jnp.int32) * grid_size + grid_at
    col_tiles = jnp.arange(tile_cols, dtype=jnp.int32) * blk_size + blk_at
    main, halo, total = stiffness_tiles(row_tiles, col_tiles, data)

    halo = lax.ppermute(halo, "blk", ring(blk_size, 1))
    totals = [lax.ppermute(total, "blk", ring(blk_size, s)) for s in range(1, blk_size)]
    total = functools.reduce(jnp.add, totals, total)
    mass = mass_windows(row_tiles, data, total)

    halo = halo.reshape(tile_rows, tile_cols // 2, WIN, 2, HALO).transpose(0, 1, 3, 2, 4)
    halo = halo.reshape(tile_rows, tile_cols, WIN, HALO)
    halo = jnp.where(blk_at == 0, jnp.roll(halo, 1, axis=1), halo)
    here = (col_tiles[None, :] == row_tiles[:, None])[:, :, None, None]
    after = (col_tiles[None, :] == (row_tiles[:, None] + 1) % tiles)[:, :, None, None]
    stiff = main + jnp.where(here, mass[:, None, :, :TB], 0.0)
    side = halo + jnp.where(after, mass[:, None, :, TB:], 0.0)
    stiff = stiff + jnp.pad(side, ((0, 0), (0, 0), (0, 0), (0, TB - HALO)))

    below = lax.ppermute(stiff[:, :, TB:, :], "grid", ring(grid_size, 1))
    below = jnp.where(grid_at == 0, jnp.roll(below, 1, axis=0), below)
    stiff = stiff[:, :, :TB, :] + jnp.pad(below, ((0, 0), (0, 0), (0, TB - HALO), (0, 0)))

    column = stiff[:, 0]
    sent = [lax.ppermute(column, "blk", [(0, j)]) for j in range(1, blk_size)]
    column = jnp.where(blk_at == 0, column, functools.reduce(jnp.add, sent))
    panel = gather_axis(column, "grid").transpose(1, 0, 2, 3).reshape(M, TB)
    head = panel[:TB]
    lower = jnp.linalg.cholesky(0.5 * (head + head.T))
    rest = lax.linalg.triangular_solve(
        lower, panel[TB:], left_side=False, lower=True, transpose_a=True
    )
    factor_cols = jnp.concatenate([lower, rest], axis=0)
    row_part = lax.dynamic_index_in_dim(
        factor_cols.reshape(tile_rows, grid_size, TB, TB), grid_at, 1, keepdims=False
    )
    col_part = lax.dynamic_index_in_dim(
        factor_cols.reshape(tile_cols, blk_size, TB, TB), blk_at, 1, keepdims=False
    )
    update = jnp.einsum("xuw,yvw->xyuv", row_part, col_part, precision=lax.Precision.HIGHEST)
    tile_row = row_tiles[:, None, None, None]
    tile_col = col_tiles[None, :, None, None]
    whole_row = tile_row * TB + jnp.arange(TB, dtype=jnp.int32)[None, None, :, None]
    whole_col = tile_col * TB + jnp.arange(TB, dtype=jnp.int32)[None, None, None, :]
    result = jnp.where(
        tile_col == 0, row_part[:, None], jnp.where(tile_row == 0, 0.0, stiff - update)
    )
    return jnp.where(whole_row >= whole_col, result, 0.0).transpose(0, 2, 1, 3)


def solution(mesh):
    in_specs = (
        P(("blk", "grid"), None),
        P(None, None, ("blk", "grid")),
        P(None, None, ("blk", "grid")),
    )
    out_specs = P(None, "grid", None, "blk")
    return jax.shard_map(shards, mesh=mesh, in_specs=in_specs, out_specs=out_specs, check_vma=False)
```

```python
import functools
import math

import jax
import jax.numpy as jnp
from jax import lax
from jax.experimental import pallas as pl
from jax.experimental.pallas import tpu as pltpu
from jax.sharding import PartitionSpec as P

M = 2048
EX = 64
EY = 32
QP = 9
TB = 128

KERNEL_GAIN = 0.02
MASS_SHIFT = 0.05

TILE_IX = TB // EY
WIN_IX = TILE_IX + 2
WIN = WIN_IX * EY
HALO = WIN - TB
COLS = 256
POINTS = QP * TB
GROUPS = 3 + QP
KROWS = 16
SUB = 3
HALF = EX / 2.0
ROUND_X = 1.5 * 2.0**23 * HALF
ROUND_Y = 1.5 * 2.0**23 * (HALF * EY / EX)


def bernstein_table():
    spread_root = 0.5 * math.sqrt(0.6)
    gauss_nodes = [0.5 - spread_root, 0.5, 0.5 + spread_root]

    def bern_poly(which, where):
        return [(1.0 - where) ** 2, 2.0 * where * (1.0 - where), where * where][which]

    table_rows = []
    for i in range(3):
        for j in range(3):
            table_row = []
            for a in range(3):
                for b in range(3):
                    table_row.append(bern_poly(a, gauss_nodes[i]) * bern_poly(b, gauss_nodes[j]))
            table_rows.append(table_row)
    return jnp.asarray(table_rows, jnp.float32)


def ring(size, shift):
    return [(i, (i + shift) % size) for i in range(size)]


def gather_axis(x, axis):
    size = lax.axis_size(axis)
    at = lax.axis_index(axis)
    got = [x] + [lax.ppermute(x, axis, ring(size, s)) for s in range(1, size)]
    back = jnp.stack(got[::-1] + got[::-1])
    return lax.dynamic_slice_in_dim(back, size - 1 - at, size, 0)


def gather_all(x):
    grid_size, blk_size = lax.axis_size("grid"), lax.axis_size("blk")
    x = jnp.stack(
        [x] + [lax.ppermute(x, "grid", ring(grid_size, 2 * s)) for s in range(1, grid_size // 2)]
    )
    x = jnp.stack([x] + [lax.ppermute(x, "blk", ring(blk_size, s)) for s in range(1, blk_size)])
    x = jnp.stack([x, lax.ppermute(x, "grid", [(i, i ^ 1) for i in range(grid_size)])])
    return x.reshape(-1, *x.shape[3:])


def gathered_order():
    grid_size, blk_size = lax.axis_size("grid"), lax.axis_size("blk")
    grid_at, blk_at = lax.axis_index("grid"), lax.axis_index("blk")
    depth = grid_size // 2
    flat = jnp.arange(blk_size * grid_size, dtype=jnp.int32)
    blk_of, grid_of = flat // grid_size, flat % grid_size
    core = grid_of % 2 ^ grid_at % 2
    return (core * blk_size + (blk_at - blk_of) % blk_size) * depth + (
        grid_at // 2 - grid_of // 2
    ) % depth


def local_pack(conn, extract, points, first):
    count = conn.shape[0]
    element = first + jnp.arange(count, dtype=jnp.int32)
    step_x = (conn // EY - (element // EY)[:, None]) % EX
    step_y = (conn % EY - (element % EY)[:, None]) % EY
    slot = (3 * step_x + step_y).T
    values = jnp.einsum("kb,abn->akn", bernstein_table(), extract, precision=lax.Precision.HIGHEST)
    names = jnp.arange(QP, dtype=jnp.int32)
    ordered = jnp.sum(
        jnp.where(slot[None, :, None, :] == names[:, None, None, None], values[None], 0.0), axis=1
    )
    scaled = jnp.concatenate([points[:2] * HALF, points[2:]], axis=0)
    flat = jnp.concatenate([scaled, ordered], axis=0).reshape(GROUPS * QP, count)
    parts = TB // count
    height = -(-GROUPS * QP // parts // 8) * 8
    flat = jnp.pad(flat, ((0, parts * height - GROUPS * QP), (0, 0)))
    return flat.reshape(parts, height, count).transpose(1, 0, 2).reshape(height, TB)


def load_tile(order, data, first, flat, tile):
    total, height, _ = data.shape
    parts = flat.shape[0] // height
    count = TB // parts
    segment = lax.broadcasted_iota(jnp.int32, (height, TB), 1) // count
    pieces = [data[order[(first + i) % total]] for i in range(parts)]
    for m in range(parts):
        rows = jnp.zeros((height, TB), jnp.float32)
        for i in range(parts):
            shift = (i - m) * count % TB
            turned = pltpu.roll(pieces[i], shift, 1) if shift else pieces[i]
            rows = jnp.where(segment == i, turned, rows)
        flat[m * height : (m + 1) * height] = rows
    tile[:, QP:, :] = jnp.zeros((GROUPS, KROWS - QP, TB), jnp.float32)
    for group in range(GROUPS):
        tile[group, :QP, :] = flat[group * QP : (group + 1) * QP, :]


def store_basis(tile, scale, hi_ref, lo_ref):
    lane = lax.broadcasted_iota(jnp.int32, (1, TB), 1)
    column = lane // EY
    fy = lax.broadcasted_iota(jnp.int32, (EY, TB), 0)
    iy = lax.broadcasted_iota(jnp.int32, (EY, TB), 1) % EY
    step = (fy - iy + EY) % EY
    masks = [step == t for t in range(3)]
    for fx in range(WIN_IX):
        hi, lo = [], []
        for t in range(3):
            rows = jnp.zeros((KROWS, TB), jnp.float32)
            for ix in range(TILE_IX):
                if 0 <= fx - ix < 3:
                    rows = jnp.where(column == ix, tile[3 + 3 * (fx - ix) + t], rows)
            rows = rows * scale
            top = rows.astype(jnp.bfloat16).astype(jnp.float32)
            hi.append(top)
            lo.append(rows - top)
        for k in range(QP):
            for parts, ref in ((hi, hi_ref), (lo, lo_ref)):
                block = jnp.zeros((EY, TB), jnp.float32)
                for t in range(3):
                    block = jnp.where(masks[t], parts[t][k : k + 1], block)
                ref[fx * EY : (fx + 1) * EY, k * TB : (k + 1) * TB] = block.astype(jnp.bfloat16)


def store_weight(tile, hi_ref, lo_ref):
    first = lax.broadcasted_iota(jnp.int32, (COLS - WIN, TB), 0) == 0
    rows = tile[2]
    top = rows.astype(jnp.bfloat16).astype(jnp.float32)
    for k in range(QP):
        for part, ref in ((top, hi_ref), (rows - top, lo_ref)):
            block = jnp.where(first, part[k : k + 1], 0.0)
            ref[WIN:, k * TB : (k + 1) * TB] = block.astype(jnp.bfloat16)


def nt(a, b):
    return lax.dot_general(a, b, (((1,), (1,)), ((), ())), preferred_element_type=jnp.float32)


def nn(a, b):
    return lax.dot_general(a, b, (((1,), (0,)), ((), ())), preferred_element_type=jnp.float32)


def kernel_block(xp, yp, xq, yq):
    gx = xp - xq
    gx = gx - ((gx + ROUND_X) - ROUND_X)
    gy = yp - yq
    gy = gy - ((gy + ROUND_Y) - ROUND_Y)
    inverse = lax.rsqrt(gx * gx + gy * gy + 1.0)
    square = inverse * inverse
    return square * square * lax.rsqrt(inverse)


def store_columns(row, ref, at):
    ref[at : at + TB, :] = jnp.broadcast_to(row, (TB, TB)).T


def tile_body(
    tile_cols, last, rows_ref, cols_ref, order, data, main_ref, halo_ref, total_ref,
    flat, rtile, ctile, xp_ref, yp_ref, rhi, rlo, chi, clo, ghi, pot,
):
    t = pl.program_id(0)
    c = t % tile_cols
    before = (t + tile_cols - 1) % tile_cols
    parts = flat.shape[0] // data.shape[1]
    step_rows = 32
    blocks = QP // SUB

    def evaluate(block):
        for i in range(SUB * TB // step_rows):
            at = block * SUB * TB + i * step_rows
            xp = xp_ref[at : at + step_rows, :]
            yp = yp_ref[at : at + step_rows, :]
            for k in range(QP):
                g = kernel_block(xp, yp, ctile[0, k : k + 1, :], ctile[1, k : k + 1, :])
                ghi[block, i * step_rows : (i + 1) * step_rows, k * TB : (k + 1) * TB] = g.astype(
                    jnp.bfloat16
                )

    def contract(block):
        slot = block
        pot[block * SUB * TB : (block + 1) * SUB * TB, :] = nt(ghi[slot], chi[...]) + nt(
            ghi[slot], clo[...]
        )

    def finish():
        for k in range(QP):
            turned = pot[k * TB : (k + 1) * TB, TB:].T
            old = jnp.where(before == 0, 0.0, total_ref[0, k : k + 1, :])
            total_ref[0, k : k + 1, :] = old + KERNEL_GAIN * turned[HALO : HALO + 1, :]
        total_ref[0, QP:, :] = jnp.zeros((KROWS - QP, TB), jnp.float32)
        full = pot[...]
        top = full.astype(jnp.bfloat16)
        rest = (full - top.astype(jnp.float32)).astype(jnp.bfloat16)
        stiff = -KERNEL_GAIN * (nn(rhi[...], top) + nn(rlo[...], top) + nn(rhi[...], rest))
        main_ref[0, 0] = stiff[:, :TB]
        halo_ref[0, 0] = stiff[:, TB:]

    @pl.when(jnp.logical_and(t < last, c == 0))
    def _():
        load_tile(order, data, rows_ref[t // tile_cols] * parts, flat, rtile)
        for k in range(QP):
            store_columns(rtile[0, k : k + 1, :], xp_ref, k * TB)
            store_columns(rtile[1, k : k + 1, :], yp_ref, k * TB)

    @pl.when(t < last)
    def _():
        load_tile(order, data, cols_ref[c] * parts, flat, ctile)
        evaluate(0)
        contract(blocks - 1)
        store_basis(ctile, ctile[2], chi, clo)
        store_weight(ctile, chi, clo)
        evaluate(1)
        finish()
        contract(0)
        evaluate(2)
        contract(1)

    @pl.when(jnp.logical_and(t < last, c == 0))
    def _():
        store_basis(rtile, rtile[2], rhi, rlo)

    @pl.when(t == last)
    def _():
        contract(blocks - 1)
        finish()


def stiffness_tiles(row_tiles, col_tiles, order, data):
    tile_rows, tile_cols = row_tiles.shape[0], col_tiles.shape[0]
    count = M // data.shape[0]
    flat_rows = TB // count * data.shape[1]
    last = tile_rows * tile_cols
    f32, b16 = jnp.float32, jnp.bfloat16

    def done(t):
        return jnp.maximum(t - 1, 0)

    return pl.pallas_call(
        functools.partial(tile_body, tile_cols, last),
        out_shape=(
            jax.ShapeDtypeStruct((tile_rows, tile_cols, WIN, TB), f32),
            jax.ShapeDtypeStruct((tile_rows, tile_cols, WIN, TB), f32),
            jax.ShapeDtypeStruct((tile_rows, KROWS, TB), f32),
        ),
        grid_spec=pltpu.PrefetchScalarGridSpec(
            num_scalar_prefetch=3,
            grid=(last + 1,),
            in_specs=[pl.BlockSpec(data.shape, lambda t, *_: (0, 0, 0))],
            out_specs=(
                pl.BlockSpec((1, 1, WIN, TB), lambda t, *_: (done(t) // tile_cols, done(t) % tile_cols, 0, 0)),
                pl.BlockSpec((1, 1, WIN, TB), lambda t, *_: (done(t) // tile_cols, done(t) % tile_cols, 0, 0)),
                pl.BlockSpec((1, KROWS, TB), lambda t, *_: (done(t) // tile_cols, 0, 0)),
            ),
            scratch_shapes=[
                pltpu.VMEM((flat_rows, TB), f32),
                pltpu.VMEM((GROUPS, KROWS, TB), f32),
                pltpu.VMEM((GROUPS, KROWS, TB), f32),
                pltpu.VMEM((POINTS, TB), f32),
                pltpu.VMEM((POINTS, TB), f32),
                pltpu.VMEM((WIN, POINTS), b16),
                pltpu.VMEM((WIN, POINTS), b16),
                pltpu.VMEM((COLS, POINTS), b16),
                pltpu.VMEM((COLS, POINTS), b16),
                pltpu.VMEM((QP // SUB, SUB * TB, POINTS), b16),
                pltpu.VMEM((POINTS, COLS), f32),
            ],
        ),
        compiler_params=pltpu.CompilerParams(dimension_semantics=("arbitrary",)),
    )(row_tiles, col_tiles, order, data)


def mass_body(rows_ref, order, data, total_ref, mass_ref, flat, tile, lhi, llo, bhi, blo):
    parts = flat.shape[0] // data.shape[1]
    load_tile(order, data, rows_ref[pl.program_id(0)] * parts, flat, tile)
    store_basis(tile, tile[2] * (MASS_SHIFT + total_ref[0]), lhi, llo)
    store_basis(tile, jnp.ones((KROWS, TB), jnp.float32), bhi, blo)
    mass_ref[0] = nt(lhi[...], bhi[...]) + nt(llo[...], bhi[...]) + nt(lhi[...], blo[...])


def mass_windows(row_tiles, order, data, total):
    tile_rows = row_tiles.shape[0]
    flat_rows = TB // (M // data.shape[0]) * data.shape[1]
    return pl.pallas_call(
        mass_body,
        out_shape=jax.ShapeDtypeStruct((tile_rows, WIN, WIN), jnp.float32),
        grid_spec=pltpu.PrefetchScalarGridSpec(
            num_scalar_prefetch=2,
            grid=(tile_rows,),
            in_specs=[
                pl.BlockSpec(data.shape, lambda r, *_: (0, 0, 0)),
                pl.BlockSpec((1, KROWS, TB), lambda r, *_: (r, 0, 0)),
            ],
            out_specs=pl.BlockSpec((1, WIN, WIN), lambda r, *_: (r, 0, 0)),
            scratch_shapes=[
                pltpu.VMEM((flat_rows, TB), jnp.float32),
                pltpu.VMEM((GROUPS, KROWS, TB), jnp.float32),
            ]
            + [pltpu.VMEM((WIN, POINTS), jnp.bfloat16)] * 4,
        ),
        compiler_params=pltpu.CompilerParams(dimension_semantics=("arbitrary",)),
    )(row_tiles, order, data, total)


def shards(conn, extract, points):
    count = conn.shape[0]
    grid_size = lax.axis_size("grid")
    blk_size = lax.axis_size("blk")
    grid_at = lax.axis_index("grid")
    blk_at = lax.axis_index("blk")
    tiles = M // TB
    tile_rows = tiles // grid_size
    tile_cols = tiles // blk_size

    own = local_pack(conn, extract, points, (blk_at * grid_size + grid_at) * count)
    data = gather_all(own)
    order = gathered_order()

    row_tiles = jnp.arange(tile_rows, dtype=jnp.int32) * grid_size + grid_at
    col_tiles = jnp.arange(tile_cols, dtype=jnp.int32) * blk_size + blk_at
    main, halo, total = stiffness_tiles(row_tiles, col_tiles, order, data)

    pairs = halo.reshape(tile_rows, tile_cols // 2, 2, WIN, TB)[..., :HALO]
    halo = jnp.concatenate([pairs[:, :, 0], pairs[:, :, 1]], axis=-1)
    halo = lax.ppermute(halo, "blk", ring(blk_size, 1))
    totals = [lax.ppermute(total, "blk", ring(blk_size, s)) for s in range(1, blk_size)]
    total = functools.reduce(jnp.add, totals, total)
    mass = mass_windows(row_tiles, order, data, total)

    halo = jnp.stack([halo[..., :HALO], halo[..., HALO:]], axis=2)
    halo = halo.reshape(tile_rows, tile_cols, WIN, HALO)
    halo = jnp.where(blk_at == 0, jnp.roll(halo, 1, axis=1), halo)
    here = (col_tiles[None, :] == row_tiles[:, None])[:, :, None, None]
    after = (col_tiles[None, :] == (row_tiles[:, None] + 1) % tiles)[:, :, None, None]
    stiff = main + jnp.where(here, mass[:, None, :, :TB], 0.0)
    side = halo + jnp.where(after, mass[:, None, :, TB:], 0.0)
    stiff = stiff + jnp.pad(side, ((0, 0), (0, 0), (0, 0), (0, TB - HALO)))

    below = lax.ppermute(stiff[:, :, TB:, :], "grid", ring(grid_size, 1))
    below = jnp.where(grid_at == 0, jnp.roll(below, 1, axis=0), below)
    stiff = stiff[:, :, :TB, :] + jnp.pad(below, ((0, 0), (0, 0), (0, TB - HALO), (0, 0)))

    column = stiff[:, 0]
    sent = [lax.ppermute(column, "blk", [(0, j)]) for j in range(1, blk_size)]
    column = jnp.where(blk_at == 0, column, functools.reduce(jnp.add, sent))
    panel = gather_axis(column, "grid").transpose(1, 0, 2, 3).reshape(M, TB)
    head = panel[:TB]
    lower = jnp.linalg.cholesky(0.5 * (head + head.T))
    rest = lax.linalg.triangular_solve(
        lower, panel[TB:], left_side=False, lower=True, transpose_a=True
    )
    factor_cols = jnp.concatenate([lower, rest], axis=0)
    row_part = lax.dynamic_index_in_dim(
        factor_cols.reshape(tile_rows, grid_size, TB, TB), grid_at, 1, keepdims=False
    )
    col_part = lax.dynamic_index_in_dim(
        factor_cols.reshape(tile_cols, blk_size, TB, TB), blk_at, 1, keepdims=False
    )
    update = jnp.einsum("xuw,yvw->xyuv", row_part, col_part, precision=lax.Precision.HIGHEST)
    tile_row = row_tiles[:, None, None, None]
    tile_col = col_tiles[None, :, None, None]
    whole_row = tile_row * TB + jnp.arange(TB, dtype=jnp.int32)[None, None, :, None]
    whole_col = tile_col * TB + jnp.arange(TB, dtype=jnp.int32)[None, None, None, :]
    result = jnp.where(
        tile_col == 0, row_part[:, None], jnp.where(tile_row == 0, 0.0, stiff - update)
    )
    return jnp.where(whole_row >= whole_col, result, 0.0).transpose(0, 2, 1, 3)


def solution(mesh):
    in_specs = (
        P(("blk", "grid"), None),
        P(None, None, ("blk", "grid")),
        P(None, None, ("blk", "grid")),
    )
    out_specs = P(None, "grid", None, "blk")
    return jax.shard_map(shards, mesh=mesh, in_specs=in_specs, out_specs=out_specs, check_vma=False)
```

```python
import functools
import math

import jax
import jax.numpy as jnp
from jax import lax
from jax.experimental import pallas as pl
from jax.experimental.pallas import tpu as pltpu
from jax.sharding import PartitionSpec as P

M = 2048
EX = 64
EY = 32
QP = 9
TB = 128

KERNEL_GAIN = 0.02
MASS_SHIFT = 0.05

TILE_IX = TB // EY
WIN_IX = TILE_IX + 2
WIN = WIN_IX * EY
HALO = WIN - TB
COLS = 256
POINTS = QP * TB
GROUPS = 3 + QP
KROWS = 16
SIDE = POINTS // 2
STRIP = SIDE // 3
REACH = TILE_IX + 7
HALF = EX / 2.0
ROUND_X = 1.5 * 2.0**23 * HALF
ROUND_Y = 1.5 * 2.0**23 * (HALF * EY / EX)


def bernstein_table():
    spread_root = 0.5 * math.sqrt(0.6)
    gauss_nodes = [0.5 - spread_root, 0.5, 0.5 + spread_root]

    def bern_poly(which, where):
        return [(1.0 - where) ** 2, 2.0 * where * (1.0 - where), where * where][which]

    table_rows = []
    for i in range(3):
        for j in range(3):
            table_row = []
            for a in range(3):
                for b in range(3):
                    table_row.append(bern_poly(a, gauss_nodes[i]) * bern_poly(b, gauss_nodes[j]))
            table_rows.append(table_row)
    return jnp.asarray(table_rows, jnp.float32)


def ring(size, shift):
    return [(i, (i + shift) % size) for i in range(size)]


def gather_axis(x, axis):
    size = lax.axis_size(axis)
    at = lax.axis_index(axis)
    got = [x] + [lax.ppermute(x, axis, ring(size, s)) for s in range(1, size)]
    back = jnp.stack(got[::-1] + got[::-1])
    return lax.dynamic_slice_in_dim(back, size - 1 - at, size, 0)


def gather_all(x):
    grid_size, blk_size = lax.axis_size("grid"), lax.axis_size("blk")
    x = jnp.stack(
        [x] + [lax.ppermute(x, "grid", ring(grid_size, 2 * s)) for s in range(1, grid_size // 2)]
    )
    x = jnp.stack([x] + [lax.ppermute(x, "blk", ring(blk_size, s)) for s in range(1, blk_size)])
    x = jnp.stack([x, lax.ppermute(x, "grid", [(i, i ^ 1) for i in range(grid_size)])])
    return x.reshape(-1, *x.shape[3:])


def gathered_order():
    grid_size, blk_size = lax.axis_size("grid"), lax.axis_size("blk")
    grid_at, blk_at = lax.axis_index("grid"), lax.axis_index("blk")
    depth = grid_size // 2
    flat = jnp.arange(blk_size * grid_size, dtype=jnp.int32)
    blk_of, grid_of = flat // grid_size, flat % grid_size
    core = grid_of % 2 ^ grid_at % 2
    return (core * blk_size + (blk_at - blk_of) % blk_size) * depth + (
        grid_at // 2 - grid_of // 2
    ) % depth


def local_pack(conn, extract, points, first):
    count = conn.shape[0]
    element = first + jnp.arange(count, dtype=jnp.int32)
    step_x = (conn // EY - (element // EY)[:, None]) % EX
    step_y = (conn % EY - (element % EY)[:, None]) % EY
    slot = (3 * step_x + step_y).T
    values = jnp.einsum("kb,abn->akn", bernstein_table(), extract, precision=lax.Precision.HIGHEST)
    names = jnp.arange(QP, dtype=jnp.int32)
    ordered = jnp.sum(
        jnp.where(slot[None, :, None, :] == names[:, None, None, None], values[None], 0.0), axis=1
    )
    scaled = jnp.concatenate([points[:2] * HALF, points[2:]], axis=0)
    flat = jnp.concatenate([scaled, ordered], axis=0).reshape(GROUPS * QP, count)
    parts = TB // count
    height = -(-GROUPS * QP // parts // 8) * 8
    flat = jnp.pad(flat, ((0, parts * height - GROUPS * QP), (0, 0)))
    return flat.reshape(parts, height, count).transpose(1, 0, 2).reshape(height, TB)


def load_tile(order, data, first, flat, tile):
    total, height, _ = data.shape
    parts = flat.shape[0] // height
    count = TB // parts
    segment = lax.broadcasted_iota(jnp.int32, (height, TB), 1) // count
    pieces = [data[order[(first + i) % total]] for i in range(parts)]
    for m in range(parts):
        rows = jnp.zeros((height, TB), jnp.float32)
        for i in range(parts):
            shift = (i - m) * count % TB
            turned = pltpu.roll(pieces[i], shift, 1) if shift else pieces[i]
            rows = jnp.where(segment == i, turned, rows)
        flat[m * height : (m + 1) * height] = rows
    tile[:, QP:, :] = jnp.zeros((GROUPS, KROWS - QP, TB), jnp.float32)
    for group in range(GROUPS):
        tile[group, :QP, :] = flat[group * QP : (group + 1) * QP, :]


def store_basis(tile, scale, hi_ref, lo_ref):
    lane = lax.broadcasted_iota(jnp.int32, (1, TB), 1)
    column = lane // EY
    fy = lax.broadcasted_iota(jnp.int32, (EY, TB), 0)
    iy = lax.broadcasted_iota(jnp.int32, (EY, TB), 1) % EY
    step = (fy - iy + EY) % EY
    masks = [step == t for t in range(3)]
    for fx in range(WIN_IX):
        hi, lo = [], []
        for t in range(3):
            rows = jnp.zeros((KROWS, TB), jnp.float32)
            for ix in range(TILE_IX):
                if 0 <= fx - ix < 3:
                    rows = jnp.where(column == ix, tile[3 + 3 * (fx - ix) + t], rows)
            rows = rows * scale
            top = rows.astype(jnp.bfloat16).astype(jnp.float32)
            hi.append(top)
            lo.append(rows - top)
        for k in range(QP):
            for parts, ref in ((hi, hi_ref), (lo, lo_ref)):
                block = jnp.zeros((EY, TB), jnp.float32)
                for t in range(3):
                    block = jnp.where(masks[t], parts[t][k : k + 1], block)
                ref[fx * EY : (fx + 1) * EY, k * TB : (k + 1) * TB] = block.astype(jnp.bfloat16)


def store_weight(tile, hi_ref, lo_ref):
    first = lax.broadcasted_iota(jnp.int32, (COLS - WIN, TB), 0) == 0
    rows = tile[2]
    top = rows.astype(jnp.bfloat16).astype(jnp.float32)
    for k in range(QP):
        for part, ref in ((top, hi_ref), (rows - top, lo_ref)):
            block = jnp.where(first, part[k : k + 1], 0.0)
            ref[WIN:, k * TB : (k + 1) * TB] = block.astype(jnp.bfloat16)


def nt(a, b):
    return lax.dot_general(a, b, (((1,), (1,)), ((), ())), preferred_element_type=jnp.float32)


def nn(a, b):
    return lax.dot_general(a, b, (((1,), (0,)), ((), ())), preferred_element_type=jnp.float32)


def kernel_block(xp, yp, xq, yq, wrapped):
    gx = xp - xq
    if wrapped:
        gx = gx - ((gx + ROUND_X) - ROUND_X)
    gy = yp - yq
    gy = gy - ((gy + ROUND_Y) - ROUND_Y)
    return jnp.exp2(-1.75 * jnp.log2(gx * gx + gy * gy + 1.0))


def store_columns(row, ref, at):
    ref[at : at + TB, :] = jnp.broadcast_to(row, (TB, TB)).T


def tile_body(
    tile_cols, last, rows_ref, cols_ref, order, data, main_ref, halo_ref, total_ref,
    flat, rtile, ctile, xp_ref, yp_ref, rhi, rlo, chi, clo, gtop, gend, pot, ytop, yrest, qx,
):
    t = pl.program_id(0)
    c = t % tile_cols
    before = (t + tile_cols - 1) % tile_cols
    parts = flat.shape[0] // data.shape[1]
    busy = t < last
    step_rows = 32
    tiles = M // TB
    offset = rows_ref[jnp.minimum(t, last - 1) // tile_cols] - cols_ref[c]
    apart = jnp.abs(offset)
    unsure = jnp.logical_and(
        TILE_IX * apart + REACH > EX // 2, TILE_IX * (tiles - apart) + REACH > EX // 2
    )

    def contract(at, g_ref, i):
        rows = pl.ds(pl.multiple_of(i * STRIP, STRIP), STRIP)
        g = g_ref[rows, :]
        pot[pl.ds(pl.multiple_of(at + i * STRIP, STRIP), STRIP), :] = nt(g, chi[...]) + nt(g, clo[...])

    def sweep(at, g_ref, other, other_ref, wrapped):
        @pl.loop(0, SIDE // STRIP)
        def _(i):
            for j in range(STRIP // step_rows):
                rows = pl.ds(pl.multiple_of(at + i * STRIP + j * step_rows, step_rows), step_rows)
                into = pl.ds(pl.multiple_of(i * STRIP + j * step_rows, step_rows), step_rows)
                xp, yp = xp_ref[rows, :], yp_ref[rows, :]
                for k in range(QP):
                    g = kernel_block(xp, yp, qx[k : k + 1, :], ctile[1, k : k + 1, :], wrapped)
                    g_ref[into, k * TB : (k + 1) * TB] = g.astype(jnp.bfloat16)
            contract(other, other_ref, i)

    def split():
        for k in range(QP):
            turned = pot[k * TB : (k + 1) * TB, TB:].T
            old = jnp.where(before == 0, 0.0, total_ref[0, k : k + 1, :])
            total_ref[0, k : k + 1, :] = old + KERNEL_GAIN * turned[HALO : HALO + 1, :]
        total_ref[0, QP:, :] = jnp.zeros((KROWS - QP, TB), jnp.float32)
        for k in range(QP):
            rows = slice(k * TB, (k + 1) * TB)
            full = pot[rows, :]
            top = full.astype(jnp.bfloat16)
            ytop[rows, :] = top
            yrest[rows, :] = (full - top.astype(jnp.float32)).astype(jnp.bfloat16)

    def finish():
        stiff = nn(rhi[...], ytop[...]) + nn(rlo[...], ytop[...]) + nn(rhi[...], yrest[...])
        main_ref[0, 0] = -KERNEL_GAIN * stiff[:, :TB]
        halo_ref[0, 0] = -KERNEL_GAIN * stiff[:, TB:]

    @pl.when(jnp.logical_and(busy, c == 0))
    def _():
        load_tile(order, data, rows_ref[t // tile_cols] * parts, flat, rtile)
        for k in range(QP):
            store_columns(rtile[0, k : k + 1, :], xp_ref, k * TB)
            store_columns(rtile[1, k : k + 1, :], yp_ref, k * TB)

    @pl.when(busy)
    def _():
        load_tile(order, data, cols_ref[c] * parts, flat, ctile)
        image = jnp.where(unsure, 0, (2 * offset > tiles).astype(jnp.int32) - (2 * offset < -tiles).astype(jnp.int32))
        qx[...] = ctile[0] + image.astype(jnp.float32) * HALF

    for wrapped in (False, True):

        @pl.when(jnp.logical_and(busy, unsure == wrapped))
        def _(wrapped=wrapped):
            sweep(0, gtop, SIDE, gend, wrapped)

    @pl.when(busy)
    def _():
        split()
        store_basis(ctile, ctile[2], chi, clo)
        store_weight(ctile, chi, clo)
        finish()

    for wrapped in (False, True):

        @pl.when(jnp.logical_and(busy, unsure == wrapped))
        def _(wrapped=wrapped):
            sweep(SIDE, gend, 0, gtop, wrapped)

    @pl.when(jnp.logical_and(busy, c == 0))
    def _():
        store_basis(rtile, rtile[2], rhi, rlo)

    @pl.when(t == last)
    def _():
        @pl.loop(0, SIDE // STRIP)
        def _(i):
            contract(SIDE, gend, i)

        split()
        finish()


def stiffness_tiles(row_tiles, col_tiles, order, data):
    tile_rows, tile_cols = row_tiles.shape[0], col_tiles.shape[0]
    count = M // data.shape[0]
    flat_rows = TB // count * data.shape[1]
    last = tile_rows * tile_cols
    f32, b16 = jnp.float32, jnp.bfloat16

    def done(t):
        return jnp.maximum(t - 1, 0)

    return pl.pallas_call(
        functools.partial(tile_body, tile_cols, last),
        out_shape=(
            jax.ShapeDtypeStruct((tile_rows, tile_cols, WIN, TB), f32),
            jax.ShapeDtypeStruct((tile_rows, tile_cols, WIN, TB), f32),
            jax.ShapeDtypeStruct((tile_rows, KROWS, TB), f32),
        ),
        grid_spec=pltpu.PrefetchScalarGridSpec(
            num_scalar_prefetch=3,
            grid=(last + 1,),
            in_specs=[pl.BlockSpec(data.shape, lambda t, *_: (0, 0, 0))],
            out_specs=(
                pl.BlockSpec((1, 1, WIN, TB), lambda t, *_: (done(t) // tile_cols, done(t) % tile_cols, 0, 0)),
                pl.BlockSpec((1, 1, WIN, TB), lambda t, *_: (done(t) // tile_cols, done(t) % tile_cols, 0, 0)),
                pl.BlockSpec((1, KROWS, TB), lambda t, *_: (done(t) // tile_cols, 0, 0)),
            ),
            scratch_shapes=[
                pltpu.VMEM((flat_rows, TB), f32),
                pltpu.VMEM((GROUPS, KROWS, TB), f32),
                pltpu.VMEM((GROUPS, KROWS, TB), f32),
                pltpu.VMEM((POINTS, TB), f32),
                pltpu.VMEM((POINTS, TB), f32),
                pltpu.VMEM((WIN, POINTS), b16),
                pltpu.VMEM((WIN, POINTS), b16),
                pltpu.VMEM((COLS, POINTS), b16),
                pltpu.VMEM((COLS, POINTS), b16),
                pltpu.VMEM((SIDE, POINTS), b16),
                pltpu.VMEM((SIDE, POINTS), b16),
                pltpu.VMEM((POINTS, COLS), f32),
                pltpu.VMEM((POINTS, COLS), b16),
                pltpu.VMEM((POINTS, COLS), b16),
                pltpu.VMEM((KROWS, TB), f32),
            ],
        ),
        compiler_params=pltpu.CompilerParams(dimension_semantics=("arbitrary",)),
    )(row_tiles, col_tiles, order, data)


def mass_body(rows_ref, order, data, total_ref, mass_ref, flat, tile, lhi, llo, bhi, blo):
    parts = flat.shape[0] // data.shape[1]
    load_tile(order, data, rows_ref[pl.program_id(0)] * parts, flat, tile)
    store_basis(tile, tile[2] * (MASS_SHIFT + total_ref[0]), lhi, llo)
    store_basis(tile, jnp.ones((KROWS, TB), jnp.float32), bhi, blo)
    mass_ref[0] = nt(lhi[...], bhi[...]) + nt(llo[...], bhi[...]) + nt(lhi[...], blo[...])


def mass_windows(row_tiles, order, data, total):
    tile_rows = row_tiles.shape[0]
    flat_rows = TB // (M // data.shape[0]) * data.shape[1]
    return pl.pallas_call(
        mass_body,
        out_shape=jax.ShapeDtypeStruct((tile_rows, WIN, WIN), jnp.float32),
        grid_spec=pltpu.PrefetchScalarGridSpec(
            num_scalar_prefetch=2,
            grid=(tile_rows,),
            in_specs=[
                pl.BlockSpec(data.shape, lambda r, *_: (0, 0, 0)),
                pl.BlockSpec((1, KROWS, TB), lambda r, *_: (r, 0, 0)),
            ],
            out_specs=pl.BlockSpec((1, WIN, WIN), lambda r, *_: (r, 0, 0)),
            scratch_shapes=[
                pltpu.VMEM((flat_rows, TB), jnp.float32),
                pltpu.VMEM((GROUPS, KROWS, TB), jnp.float32),
            ]
            + [pltpu.VMEM((WIN, POINTS), jnp.bfloat16)] * 4,
        ),
        compiler_params=pltpu.CompilerParams(dimension_semantics=("arbitrary",)),
    )(row_tiles, order, data, total)


def shards(conn, extract, points):
    count = conn.shape[0]
    grid_size = lax.axis_size("grid")
    blk_size = lax.axis_size("blk")
    grid_at = lax.axis_index("grid")
    blk_at = lax.axis_index("blk")
    tiles = M // TB
    tile_rows = tiles // grid_size
    tile_cols = tiles // blk_size

    own = local_pack(conn, extract, points, (blk_at * grid_size + grid_at) * count)
    data = gather_all(own)
    order = gathered_order()

    row_tiles = jnp.arange(tile_rows, dtype=jnp.int32) * grid_size + grid_at
    col_tiles = jnp.arange(tile_cols, dtype=jnp.int32) * blk_size + blk_at
    main, halo, total = stiffness_tiles(row_tiles, col_tiles, order, data)

    pairs = halo.reshape(tile_rows, tile_cols // 2, 2, WIN, TB)[..., :HALO]
    halo = jnp.concatenate([pairs[:, :, 0], pairs[:, :, 1]], axis=-1)
    halo = lax.ppermute(halo, "blk", ring(blk_size, 1))
    totals = [lax.ppermute(total, "blk", ring(blk_size, s)) for s in range(1, blk_size)]
    total = functools.reduce(jnp.add, totals, total)
    mass = mass_windows(row_tiles, order, data, total)

    halo = jnp.stack([halo[..., :HALO], halo[..., HALO:]], axis=2)
    halo = halo.reshape(tile_rows, tile_cols, WIN, HALO)
    halo = jnp.where(blk_at == 0, jnp.roll(halo, 1, axis=1), halo)
    here = (col_tiles[None, :] == row_tiles[:, None])[:, :, None, None]
    after = (col_tiles[None, :] == (row_tiles[:, None] + 1) % tiles)[:, :, None, None]
    stiff = main + jnp.where(here, mass[:, None, :, :TB], 0.0)
    side = halo + jnp.where(after, mass[:, None, :, TB:], 0.0)
    stiff = stiff + jnp.pad(side, ((0, 0), (0, 0), (0, 0), (0, TB - HALO)))

    below = lax.ppermute(stiff[:, :, TB:, :], "grid", ring(grid_size, 1))
    below = jnp.where(grid_at == 0, jnp.roll(below, 1, axis=0), below)
    stiff = stiff[:, :, :TB, :] + jnp.pad(below, ((0, 0), (0, 0), (0, TB - HALO), (0, 0)))

    column = stiff[:, 0]
    sent = [lax.ppermute(column, "blk", [(0, j)]) for j in range(1, blk_size)]
    column = jnp.where(blk_at == 0, column, functools.reduce(jnp.add, sent))
    panel = gather_axis(column, "grid").transpose(1, 0, 2, 3).reshape(M, TB)
    head = panel[:TB]
    lower = jnp.linalg.cholesky(0.5 * (head + head.T))
    rest = lax.linalg.triangular_solve(
        lower, panel[TB:], left_side=False, lower=True, transpose_a=True
    )
    factor_cols = jnp.concatenate([lower, rest], axis=0)
    row_part = lax.dynamic_index_in_dim(
        factor_cols.reshape(tile_rows, grid_size, TB, TB), grid_at, 1, keepdims=False
    )
    col_part = lax.dynamic_index_in_dim(
        factor_cols.reshape(tile_cols, blk_size, TB, TB), blk_at, 1, keepdims=False
    )
    update = jnp.einsum("xuw,yvw->xyuv", row_part, col_part, precision=lax.Precision.HIGHEST)
    tile_row = row_tiles[:, None, None, None]
    tile_col = col_tiles[None, :, None, None]
    whole_row = tile_row * TB + jnp.arange(TB, dtype=jnp.int32)[None, None, :, None]
    whole_col = tile_col * TB + jnp.arange(TB, dtype=jnp.int32)[None, None, None, :]
    result = jnp.where(
        tile_col == 0, row_part[:, None], jnp.where(tile_row == 0, 0.0, stiff - update)
    )
    return jnp.where(whole_row >= whole_col, result, 0.0).transpose(0, 2, 1, 3)


def solution(mesh):
    in_specs = (
        P(("blk", "grid"), None),
        P(None, None, ("blk", "grid")),
        P(None, None, ("blk", "grid")),
    )
    out_specs = P(None, "grid", None, "blk")
    return jax.shard_map(shards, mesh=mesh, in_specs=in_specs, out_specs=out_specs, check_vma=False)
```

```python
import functools
import math

import jax
import jax.numpy as jnp
from jax import lax
from jax.experimental import pallas as pl
from jax.experimental.pallas import tpu as pltpu
from jax.sharding import PartitionSpec as P


M = 2048
EX = 64
EY = 32
QP = 9
TB = 128

KERNEL_GAIN = 0.02
MASS_SHIFT = 0.05

TILE_IX = TB // EY
WIN_IX = TILE_IX + 2
WIN = WIN_IX * EY
HALO = WIN - TB
COLS = 256
POINTS = QP * TB
GROUPS = 3 + QP
KROWS = 16
GRANT = 24 << 20
UNIT = 2 * EY
EXTRA = (QP + 1) // 2
SIDE = POINTS // 2
STRIP = SIDE // 3
REACH = TILE_IX + 7
HALF = EX / 2.0
ROUND_X = 1.5 * 2.0**23 * HALF
ROUND_Y = 1.5 * 2.0**23 * (HALF * EY / EX)


def bernstein_table():
    spread_root = 0.5 * math.sqrt(0.6)
    gauss_nodes = [0.5 - spread_root, 0.5, 0.5 + spread_root]

    def bern_poly(which, where):
        return [(1.0 - where) ** 2, 2.0 * where * (1.0 - where), where * where][which]

    table_rows = []
    for i in range(3):
        for j in range(3):
            table_row = []
            for a in range(3):
                for b in range(3):
                    table_row.append(bern_poly(a, gauss_nodes[i]) * bern_poly(b, gauss_nodes[j]))
            table_rows.append(table_row)
    return jnp.asarray(table_rows, jnp.float32)


def ring(size, shift):
    return [(i, (i + shift) % size) for i in range(size)]


def gather_z(x):
    size = lax.axis_size("grid")
    return jnp.stack([x] + [lax.ppermute(x, "grid", ring(size, 2 * s)) for s in range(1, size // 2)])


def gather_blk(x):
    size = lax.axis_size("blk")
    return jnp.stack([x] + [lax.ppermute(x, "blk", ring(size, s)) for s in range(1, size)])


def gather_core(x):
    size = lax.axis_size("grid")
    x = x.reshape(-1, *x.shape[2:])
    return x, lax.ppermute(x, "grid", [(i, i ^ 1) for i in range(size)])


def fetch(near, far, place):
    depth = near.shape[0]
    return jnp.where(place < depth, near[place % depth], far[place % depth])


def gathered_order():
    grid_size, blk_size = lax.axis_size("grid"), lax.axis_size("blk")
    grid_at, blk_at = lax.axis_index("grid"), lax.axis_index("blk")
    depth = grid_size // 2
    flat = jnp.arange(blk_size * grid_size, dtype=jnp.int32)
    blk_of, grid_of = flat // grid_size, flat % grid_size
    core = grid_of % 2 ^ grid_at % 2
    return (core * blk_size + (blk_at - blk_of) % blk_size) * depth + (
        grid_at // 2 - grid_of // 2
    ) % depth


def local_pack(conn, extract, points, first):
    count = conn.shape[0]
    element = first + jnp.arange(count, dtype=jnp.int32)
    step_x = (conn // EY - (element // EY)[:, None]) % EX
    step_y = (conn % EY - (element % EY)[:, None]) % EY
    slot = (3 * step_x + step_y).T
    values = jnp.einsum("kb,abn->akn", bernstein_table(), extract, precision=lax.Precision.HIGHEST)
    names = jnp.arange(QP, dtype=jnp.int32)
    ordered = jnp.sum(
        jnp.where(slot[None, :, None, :] == names[:, None, None, None], values[None], 0.0), axis=1
    )
    scaled = jnp.concatenate([points[:2] * HALF, points[2:]], axis=0)
    flat = jnp.concatenate([scaled, ordered], axis=0).reshape(GROUPS * QP, count)
    parts = TB // count
    height = -(-GROUPS * QP // parts // 8) * 8
    flat = jnp.pad(flat, ((0, parts * height - GROUPS * QP), (0, 0)))
    return flat.reshape(parts, height, count).transpose(1, 0, 2).reshape(height, TB)


def load_tile(order, near, far, first, flat, tile):
    total, height = 2 * near.shape[0], near.shape[1]
    parts = flat.shape[0] // height
    count = TB // parts
    segment = lax.broadcasted_iota(jnp.int32, (height, TB), 1) // count
    pieces = [fetch(near, far, order[(first + i) % total]) for i in range(parts)]
    for m in range(parts):
        rows = jnp.zeros((height, TB), jnp.float32)
        for i in range(parts):
            shift = (i - m) * count % TB
            turned = pltpu.roll(pieces[i], shift, 1) if shift else pieces[i]
            rows = jnp.where(segment == i, turned, rows)
        flat[m * height : (m + 1) * height] = rows
    tile[:, QP:, :] = jnp.zeros((GROUPS, KROWS - QP, TB), jnp.float32)
    for group in range(GROUPS):
        tile[group, :QP, :] = flat[group * QP : (group + 1) * QP, :]


def store_basis(tile, scale, hi_ref, lo_ref, columns=range(WIN_IX)):
    lane = lax.broadcasted_iota(jnp.int32, (1, TB), 1)
    column = lane // EY
    fy = lax.broadcasted_iota(jnp.int32, (EY, TB), 0)
    iy = lax.broadcasted_iota(jnp.int32, (EY, TB), 1) % EY
    step = (fy - iy + EY) % EY
    masks = [step == t for t in range(3)]
    for place, fx in enumerate(columns):
        hi, lo = [], []
        for t in range(3):
            rows = jnp.zeros((KROWS, TB), jnp.float32)
            for ix in range(TILE_IX):
                if 0 <= fx - ix < 3:
                    rows = jnp.where(column == ix, tile[3 + 3 * (fx - ix) + t], rows)
            rows = rows * scale
            top = rows.astype(jnp.bfloat16).astype(jnp.float32)
            hi.append(top)
            lo.append(rows - top)
        for k in range(QP):
            for parts, ref in ((hi, hi_ref), (lo, lo_ref)):
                block = jnp.zeros((EY, TB), jnp.float32)
                for t in range(3):
                    block = jnp.where(masks[t], parts[t][k : k + 1], block)
                ref[place * EY : (place + 1) * EY, k * TB : (k + 1) * TB] = block.astype(jnp.bfloat16)


def store_weight(tile, hi_ref, lo_ref):
    first = lax.broadcasted_iota(jnp.int32, (COLS - WIN, TB), 0) == 0
    rows = tile[2]
    top = rows.astype(jnp.bfloat16).astype(jnp.float32)
    for k in range(QP):
        for part, ref in ((top, hi_ref), (rows - top, lo_ref)):
            block = jnp.where(first, part[k : k + 1], 0.0)
            ref[WIN:, k * TB : (k + 1) * TB] = block.astype(jnp.bfloat16)


def nt(a, b):
    return lax.dot_general(a, b, (((1,), (1,)), ((), ())), preferred_element_type=jnp.float32)


def nn(a, b):
    return lax.dot_general(a, b, (((1,), (0,)), ((), ())), preferred_element_type=jnp.float32)


def kernel_block(xp, yp, xq, yq, wrapped):
    gx = xp - xq
    if wrapped:
        gx = gx - ((gx + ROUND_X) - ROUND_X)
    gy = yp - yq
    gy = gy - ((gy + ROUND_Y) - ROUND_Y)
    return jnp.exp2(-1.75 * jnp.log2(gx * gx + gy * gy + 1.0))


def store_columns(row, ref, at):
    ref[at : at + TB, :] = jnp.broadcast_to(row, (TB, TB)).T


def tile_body(
    tile_cols, last, rows_ref, cols_ref, order, near, far, main_ref, halo_ref, total_ref,
    flat, rtile, ctile, xp_ref, yp_ref, rhi, rlo, chi, clo, gtop, gend, pot, ytop, yrest, qx,
):
    t = pl.program_id(0)
    c = t % tile_cols
    before = (t + tile_cols - 1) % tile_cols
    parts = flat.shape[0] // near.shape[1]
    busy = t < last
    step_rows = 32
    tiles = M // TB
    offset = rows_ref[jnp.minimum(t, last - 1) // tile_cols] - cols_ref[c]
    apart = jnp.abs(offset)
    unsure = jnp.logical_and(
        TILE_IX * apart + REACH > EX // 2, TILE_IX * (tiles - apart) + REACH > EX // 2
    )

    def contract(at, g_ref, i):
        rows = pl.ds(pl.multiple_of(i * STRIP, STRIP), STRIP)
        g = g_ref[rows, :]
        pot[pl.ds(pl.multiple_of(at + i * STRIP, STRIP), STRIP), :] = nt(g, chi[...]) + nt(g, clo[...])

    def sweep(at, g_ref, other, other_ref, wrapped):
        @pl.loop(0, SIDE // STRIP)
        def _(i):
            for j in range(STRIP // step_rows):
                rows = pl.ds(pl.multiple_of(at + i * STRIP + j * step_rows, step_rows), step_rows)
                into = pl.ds(pl.multiple_of(i * STRIP + j * step_rows, step_rows), step_rows)
                xp, yp = xp_ref[rows, :], yp_ref[rows, :]
                for k in range(QP):
                    g = kernel_block(xp, yp, qx[k : k + 1, :], ctile[1, k : k + 1, :], wrapped)
                    g_ref[into, k * TB : (k + 1) * TB] = g.astype(jnp.bfloat16)
            contract(other, other_ref, i)

    def split():
        for k in range(QP):
            turned = pot[k * TB : (k + 1) * TB, TB:].T
            old = jnp.where(before == 0, 0.0, total_ref[0, k : k + 1, :])
            total_ref[0, k : k + 1, :] = old + KERNEL_GAIN * turned[HALO : HALO + 1, :]
        total_ref[0, QP:, :] = jnp.zeros((KROWS - QP, TB), jnp.float32)
        for k in range(QP):
            rows = slice(k * TB, (k + 1) * TB)
            full = pot[rows, :]
            top = full.astype(jnp.bfloat16)
            ytop[rows, :] = top
            yrest[rows, :] = (full - top.astype(jnp.float32)).astype(jnp.bfloat16)

    def finish():
        stiff = nn(rhi[...], ytop[...]) + nn(rlo[...], ytop[...]) + nn(rhi[...], yrest[...])
        main_ref[0, 0] = -KERNEL_GAIN * stiff[:, :TB]
        halo_ref[0, 0] = -KERNEL_GAIN * stiff[:, TB:]

    @pl.when(jnp.logical_and(busy, c == 0))
    def _():
        load_tile(order, near, far, rows_ref[t // tile_cols] * parts, flat, rtile)
        for k in range(QP):
            store_columns(rtile[0, k : k + 1, :], xp_ref, k * TB)
            store_columns(rtile[1, k : k + 1, :], yp_ref, k * TB)

    @pl.when(busy)
    def _():
        load_tile(order, near, far, cols_ref[c] * parts, flat, ctile)
        image = jnp.where(unsure, 0, (2 * offset > tiles).astype(jnp.int32) - (2 * offset < -tiles).astype(jnp.int32))
        qx[...] = ctile[0] + image.astype(jnp.float32) * HALF

    for wrapped in (False, True):

        @pl.when(jnp.logical_and(busy, unsure == wrapped))
        def _(wrapped=wrapped):
            sweep(0, gtop, SIDE, gend, wrapped)

    @pl.when(busy)
    def _():
        split()
        finish()
        store_basis(ctile, ctile[2], chi, clo)
        store_weight(ctile, chi, clo)

    for wrapped in (False, True):

        @pl.when(jnp.logical_and(busy, unsure == wrapped))
        def _(wrapped=wrapped):
            sweep(SIDE, gend, 0, gtop, wrapped)

    @pl.when(jnp.logical_and(busy, c == 0))
    def _():
        store_basis(rtile, rtile[2], rhi, rlo)

    @pl.when(t == last)
    def _():
        @pl.loop(0, SIDE // STRIP)
        def _(i):
            contract(SIDE, gend, i)

        split()
        finish()


def stiffness_tiles(row_tiles, col_tiles, order, data):
    tile_rows, tile_cols = row_tiles.shape[0], col_tiles.shape[0]
    count = M // (2 * data[0].shape[0])
    flat_rows = TB // count * data[0].shape[1]
    last = tile_rows * tile_cols
    f32, b16 = jnp.float32, jnp.bfloat16

    def done(t):
        return jnp.maximum(t - 1, 0)

    return pl.pallas_call(
        functools.partial(tile_body, tile_cols, last),
        out_shape=(
            jax.ShapeDtypeStruct((tile_rows, tile_cols, WIN, TB), f32),
            jax.ShapeDtypeStruct((tile_rows, tile_cols, WIN, TB), f32),
            jax.ShapeDtypeStruct((tile_rows, KROWS, TB), f32),
        ),
        grid_spec=pltpu.PrefetchScalarGridSpec(
            num_scalar_prefetch=3,
            grid=(last + 1,),
            in_specs=[pl.BlockSpec(data[0].shape, lambda t, *_: (0, 0, 0))] * 2,
            out_specs=(
                pl.BlockSpec((1, 1, WIN, TB), lambda t, *_: (done(t) // tile_cols, done(t) % tile_cols, 0, 0)),
                pl.BlockSpec((1, 1, WIN, TB), lambda t, *_: (done(t) // tile_cols, done(t) % tile_cols, 0, 0)),
                pl.BlockSpec((1, KROWS, TB), lambda t, *_: (done(t) // tile_cols, 0, 0)),
            ),
            scratch_shapes=[
                pltpu.VMEM((flat_rows, TB), f32),
                pltpu.VMEM((GROUPS, KROWS, TB), f32),
                pltpu.VMEM((GROUPS, KROWS, TB), f32),
                pltpu.VMEM((POINTS, TB), f32),
                pltpu.VMEM((POINTS, TB), f32),
                pltpu.VMEM((WIN, POINTS), b16),
                pltpu.VMEM((WIN, POINTS), b16),
                pltpu.VMEM((COLS, POINTS), b16),
                pltpu.VMEM((COLS, POINTS), b16),
                pltpu.VMEM((SIDE, POINTS), b16),
                pltpu.VMEM((SIDE, POINTS), b16),
                pltpu.VMEM((POINTS, COLS), f32),
                pltpu.VMEM((POINTS, COLS), b16),
                pltpu.VMEM((POINTS, COLS), b16),
                pltpu.VMEM((KROWS, TB), f32),
            ],
        ),
        compiler_params=pltpu.CompilerParams(vmem_limit_bytes=GRANT),
        cost_estimate=pl.CostEstimate(
            flops=last * 2 * 10**9, bytes_accessed=2 * 10**6, transcendentals=last * 2 * POINTS**2
        ),
    )(row_tiles, col_tiles, order, *data)


def pack_half(rows):
    low = lax.broadcasted_iota(jnp.int32, (1, TB), 1) < TB // 2
    turned = pltpu.roll(rows, TB // 2, 1)
    return [
        jnp.where(low, turned[2 * m : 2 * m + 1], rows[2 * m + 1 : 2 * m + 2]) for m in range(EXTRA)
    ]


def panel_body(
    count, firsts, order, near, far, out_ref, flat, ptile, htile, ttile, xp_ref, yp_ref, phi, plain_hi, plain_lo,
    side_hi, side_lo, qx, qy, weights, gtop, gend, pot, sums, halves,
):
    parts = flat.shape[0] // near.shape[1]
    total = 2 * near.shape[0]
    load_tile(order, near, far, firsts[0], flat, ptile)
    load_tile(order, near, far, 0, flat, htile)
    load_tile(order, near, far, total - parts, flat, ttile)
    lane = lax.broadcasted_iota(jnp.int32, (1, TB), 1)
    own = jnp.logical_and(lane >= firsts[1], lane < firsts[1] + count)
    weight = jnp.where(own, ptile[2], 0.0)
    top = weight.astype(jnp.bfloat16).astype(jnp.float32)
    for k in range(QP):
        store_columns(ptile[0, k : k + 1, :], xp_ref, k * TB)
        store_columns(ptile[1, k : k + 1, :], yp_ref, k * TB)
        first = lax.broadcasted_iota(jnp.int32, (KROWS, TB), 0)
        both = jnp.where(
            first == 0, top[k : k + 1], jnp.where(first == 1, (weight - top)[k : k + 1], 0.0)
        )
        weights[k] = both.astype(jnp.bfloat16)
    for group, ref in ((0, qx), (1, qy)):
        ref[:QP, :] = htile[group, :QP, :]
        for m, row in enumerate(pack_half(ttile[group])):
            ref[QP + m : QP + m + 1, :] = row
    store_basis(htile, htile[2], plain_hi, plain_lo, range(TILE_IX))
    phi[:TB, :POINTS] = plain_hi[...]
    phi[TB:, :POINTS] = plain_lo[...]
    fy = lax.broadcasted_iota(jnp.int32, (EY, TB), 0)
    iy = lax.broadcasted_iota(jnp.int32, (EY, TB), 1) % EY
    step = (fy - iy + EY) % EY
    column = lane // EY
    phi[:, POINTS:] = jnp.zeros((2 * TB, EXTRA * TB), jnp.bfloat16)
    for place in range(WIN_IX - TILE_IX):
        fx = TILE_IX + place
        packs = []
        for t in range(3):
            rows = jnp.zeros((KROWS, TB), jnp.float32)
            for ix in range(TILE_IX):
                if 0 <= fx - ix < 3:
                    rows = jnp.where(column == ix, ttile[3 + 3 * (fx - ix) + t], rows)
            packs.append(pack_half(rows * ttile[2]))
        for m in range(EXTRA):
            block = jnp.zeros((EY, TB), jnp.float32)
            for t in range(3):
                block = jnp.where(step == t, packs[t][m], block)
            upper = block.astype(jnp.bfloat16)
            lanes = slice(POINTS + m * TB, POINTS + (m + 1) * TB)
            phi[place * EY : (place + 1) * EY, lanes] = upper
            phi[TB + place * EY : TB + (place + 1) * EY, lanes] = (
                block - upper.astype(jnp.float32)
            ).astype(jnp.bfloat16)
    store_basis(ptile, ptile[2], side_hi, side_lo, (2, 3))
    sums[...] = jnp.zeros_like(sums)
    step_rows = 32

    def evaluate(strip, g_ref):
        for j in range(TB // step_rows):
            rows = pl.ds(pl.multiple_of(strip * TB + j * step_rows, step_rows), step_rows)
            xp, yp = xp_ref[rows, :], yp_ref[rows, :]
            for k in range(QP + EXTRA):
                g = kernel_block(xp, yp, qx[k : k + 1, :], qy[k : k + 1, :], True)
                g_ref[j * step_rows : (j + 1) * step_rows, k * TB : (k + 1) * TB] = g.astype(
                    jnp.bfloat16
                )

    def contract(strip, g_ref, valid):
        g = g_ref[...]
        pot[pl.ds(pl.multiple_of(strip * TB, TB), TB), :] = nt(g, phi[...])
        sums[...] += jnp.where(valid, nn(weights[strip], g), 0.0)

    @pl.loop(0, QP // 2)
    def _(i):
        evaluate(2 * i, gtop)
        contract(jnp.maximum(2 * i - 1, 0), gend, i > 0)
        evaluate(2 * i + 1, gend)
        contract(2 * i, gtop, True)

    evaluate(QP - 1, gtop)
    contract(QP - 2, gend, True)
    contract(QP - 1, gtop, True)
    for k in range(QP):
        rows = slice(k * TB, (k + 1) * TB)
        full = pot[rows, :TB] + pot[rows, TB:]
        upper = full.astype(jnp.bfloat16)
        halves[rows, :TB] = upper
        halves[rows, TB:] = (full - upper.astype(jnp.float32)).astype(jnp.bfloat16)
    wide = nn(side_hi[...], halves[...])
    panel = wide[:, :TB] + wide[:, TB:] + nn(side_lo[...], halves[:, :TB])
    out_ref[:UNIT, :] = -KERNEL_GAIN * panel
    out_ref[UNIT:, :] = jnp.zeros((KROWS, TB), jnp.float32)
    for m in range(QP + EXTRA):
        lanes = slice(m * TB, (m + 1) * TB)
        out_ref[UNIT + m : UNIT + m + 1, :] = KERNEL_GAIN * (sums[0:1, lanes] + sums[1:2, lanes])


def panel_rows(count, firsts, order, data):
    flat_rows = TB // count * data[0].shape[1]
    f32, b16 = jnp.float32, jnp.bfloat16
    tile = pltpu.VMEM((GROUPS, KROWS, TB), f32)
    width = (QP + EXTRA) * TB
    return pl.pallas_call(
        functools.partial(panel_body, count),
        out_shape=jax.ShapeDtypeStruct((UNIT + KROWS, TB), f32),
        grid_spec=pltpu.PrefetchScalarGridSpec(
            num_scalar_prefetch=2,
            grid=(1,),
            in_specs=[pl.BlockSpec(data[0].shape, lambda i, *_: (0, 0, 0))] * 2,
            out_specs=pl.BlockSpec((UNIT + KROWS, TB), lambda i, *_: (0, 0)),
            scratch_shapes=[
                pltpu.VMEM((flat_rows, TB), f32), tile, tile, tile,
                pltpu.VMEM((POINTS, TB), f32), pltpu.VMEM((POINTS, TB), f32),
                pltpu.VMEM((2 * TB, width), b16),
                pltpu.VMEM((TB, POINTS), b16), pltpu.VMEM((TB, POINTS), b16),
                pltpu.VMEM((UNIT, POINTS), b16), pltpu.VMEM((UNIT, POINTS), b16),
                pltpu.VMEM((KROWS, TB), f32), pltpu.VMEM((KROWS, TB), f32),
                pltpu.VMEM((QP, KROWS, TB), b16),
                pltpu.VMEM((TB, width), b16), pltpu.VMEM((TB, width), b16),
                pltpu.VMEM((POINTS, 2 * TB), f32),
                pltpu.VMEM((KROWS, width), f32),
                pltpu.VMEM((POINTS, 2 * TB), b16),
            ],
        ),
        compiler_params=pltpu.CompilerParams(vmem_limit_bytes=GRANT),
        cost_estimate=pl.CostEstimate(flops=2 * 10**9, bytes_accessed=10**6, transcendentals=4 * 10**6),
    )(firsts, order, *data)


def halves_of(a):
    top = a.astype(jnp.bfloat16)
    return top, (a - top.astype(jnp.float32)).astype(jnp.bfloat16)


def cholesky_and_inverse(head):
    step = 8
    blocks = TB // step
    lane = lax.broadcasted_iota(jnp.int32, (step, TB), 1)
    sub = lax.broadcasted_iota(jnp.int32, (step, TB), 0)
    left = [head[i * step : (i + 1) * step] for i in range(blocks)]
    right = [(lane == sub + i * step).astype(jnp.float32) for i in range(blocks)]
    roots = []
    for at in range(blocks):
        later = range(at, blocks)
        column = [
            {i: jnp.broadcast_to(left[i][:, at * step + j : at * step + j + 1], (step, TB)) for i in later}
            for j in range(step)
        ]
        for row in range(step):
            pivot = jnp.broadcast_to(column[row][at][row : row + 1], (step, TB))
            scale = 1.0 / pivot
            roots.append(pivot)
            left_row = jnp.broadcast_to(left[at][row : row + 1], (step, TB)) * scale
            right_row = jnp.broadcast_to(right[at][row : row + 1], (step, TB)) * scale
            ahead = {
                j: jnp.broadcast_to(column[j][at][row : row + 1], (step, TB)) * scale
                for j in range(row + 1, step)
            }
            for i in later:
                factor = column[row][i]
                if i == at:
                    factor = jnp.where(sub > row, factor, 0.0)
                for j in range(row + 1, step):
                    column[j][i] = column[j][i] - factor * ahead[j]
                left[i] = left[i] - factor * left_row
                right[i] = right[i] - factor * right_row
    uppers, inverses = [], []
    for i in range(blocks):
        pivots = roots[i * step]
        for row in range(1, step):
            pivots = jnp.where(sub == row, roots[i * step + row], pivots)
        root = lax.rsqrt(pivots)
        uppers.append(jnp.where(lane >= sub + i * step, left[i] * root, 0.0))
        inverses.append(right[i] * root)
    return jnp.concatenate(uppers, axis=0).T, jnp.concatenate(inverses, axis=0)


def ends_body(count, order, near, far, pieces_near, pieces_far, head_mass, tail_mass, flat, tile, hi, lo):
    parts = TB // count
    total = 2 * near.shape[0]
    sums = jnp.zeros((KROWS, TB), jnp.float32)
    for d in range(total // 2):
        sums = sums + (pieces_near[d, count:, :] + pieces_far[d, count:, :])
    lane = lax.broadcasted_iota(jnp.int32, (1, TB), 1)
    turned = pltpu.roll(sums, TB // 2, 1)
    last = jnp.concatenate(
        [(turned, sums)[k % 2][QP + k // 2 : QP + k // 2 + 1] for k in range(QP)]
        + [jnp.zeros((KROWS - QP, TB), jnp.float32)],
        axis=0,
    )
    last = jnp.where(lane >= TB // 2, last, 0.0)
    for first, value, ref, cols in (
        (0, sums, head_mass, slice(0, TB)),
        (total - parts, last, tail_mass, slice(TB, WIN)),
    ):
        load_tile(order, near, far, first, flat, tile)
        store_mass(tile, value, hi, lo)
        ref[:, : cols.stop - cols.start] = (
            nt(hi[...], hi[cols, :]) + nt(lo[...], hi[cols, :]) + nt(hi[...], lo[cols, :])
        )


def end_masses(count, order, data, pieces):
    flat_rows = TB // count * data[0].shape[1]
    f32, b16 = jnp.float32, jnp.bfloat16
    basis = pltpu.VMEM((WIN, POINTS), b16)
    return pl.pallas_call(
        functools.partial(ends_body, count),
        out_shape=(jax.ShapeDtypeStruct((WIN, TB), f32), jax.ShapeDtypeStruct((WIN, TB), f32)),
        grid_spec=pltpu.PrefetchScalarGridSpec(
            num_scalar_prefetch=1,
            grid=(1,),
            in_specs=[
                pl.BlockSpec(data[0].shape, lambda i, *_: (0, 0, 0)),
                pl.BlockSpec(data[0].shape, lambda i, *_: (0, 0, 0)),
                pl.BlockSpec(pieces[0].shape, lambda i, *_: (0, 0, 0)),
                pl.BlockSpec(pieces[0].shape, lambda i, *_: (0, 0, 0)),
            ],
            out_specs=(
                pl.BlockSpec((WIN, TB), lambda i, *_: (0, 0)),
                pl.BlockSpec((WIN, TB), lambda i, *_: (0, 0)),
            ),
            scratch_shapes=[
                pltpu.VMEM((flat_rows, TB), f32), pltpu.VMEM((GROUPS, KROWS, TB), f32),
                basis, basis,
            ],
        ),
        compiler_params=pltpu.CompilerParams(vmem_limit_bytes=GRANT),
        cost_estimate=pl.CostEstimate(flops=2 * 10**9, bytes_accessed=2 * 10**6, transcendentals=0),
    )(order, *data, *pieces)


def factor_body(
    count, rows_ref, cols_ref, order, near, far, head_mass, tail_mass, rowp_ref, colp_ref, low, inverse
):
    parts = TB // count
    tiles = M // TB

    def panel_tile(index):
        rows = jnp.concatenate(
            [fetch(near, far, order[index * parts + i])[:count, :] for i in range(parts)], axis=0
        )
        side = jnp.zeros((TB, TB - HALO), jnp.float32)
        below = jnp.zeros((TB - HALO, TB), jnp.float32)
        tail = tail_mass[:, :HALO]
        corner = jnp.concatenate([tail[TB:], jnp.zeros((TB - HALO, HALO), jnp.float32)], axis=0)
        here = head_mass[:TB] + jnp.concatenate([corner, side], axis=1)
        after = jnp.concatenate([head_mass[TB:], below], axis=0)
        before = jnp.concatenate([tail[:TB], side], axis=1)
        rows = rows + jnp.where(index == 0, here, 0.0) + jnp.where(index == 1, after, 0.0)
        return rows + jnp.where(index == tiles - 1, before, 0.0)

    head = panel_tile(0)
    lower, inv = cholesky_and_inverse(0.5 * (head + head.T))
    low[...] = lower
    inverse[...] = inv
    inv_hi, inv_lo = halves_of(inverse[...])
    for ref, indices in ((rowp_ref, rows_ref), (colp_ref, cols_ref)):
        for i in range(ref.shape[0]):
            top, rest = halves_of(panel_tile(indices[i]))
            solved = nt(top, inv_hi) + nt(top, inv_lo) + nt(rest, inv_hi)
            ref[i] = jnp.where(indices[i] == 0, low[...], solved)


def panel_factor(count, row_tiles, col_tiles, order, pieces, head_mass, tail_mass):
    tile_rows, tile_cols = row_tiles.shape[0], col_tiles.shape[0]
    f32 = jnp.float32
    return pl.pallas_call(
        functools.partial(factor_body, count),
        out_shape=(
            jax.ShapeDtypeStruct((tile_rows, TB, TB), f32),
            jax.ShapeDtypeStruct((tile_cols, TB, TB), f32),
        ),
        grid_spec=pltpu.PrefetchScalarGridSpec(
            num_scalar_prefetch=3,
            grid=(1,),
            in_specs=[
                pl.BlockSpec(pieces[0].shape, lambda i, *_: (0, 0, 0)),
                pl.BlockSpec(pieces[0].shape, lambda i, *_: (0, 0, 0)),
                pl.BlockSpec((WIN, TB), lambda i, *_: (0, 0)),
                pl.BlockSpec((WIN, TB), lambda i, *_: (0, 0)),
            ],
            out_specs=(
                pl.BlockSpec((tile_rows, TB, TB), lambda i, *_: (0, 0, 0)),
                pl.BlockSpec((tile_cols, TB, TB), lambda i, *_: (0, 0, 0)),
            ),
            scratch_shapes=[pltpu.VMEM((TB, TB), f32), pltpu.VMEM((TB, TB), f32)],
        ),
        compiler_params=pltpu.CompilerParams(vmem_limit_bytes=GRANT),
        cost_estimate=pl.CostEstimate(flops=4 * 10**9, bytes_accessed=2 * 10**6, transcendentals=0),
    )(row_tiles, col_tiles, order, *pieces, head_mass, tail_mass)


def store_mass(tile, total, hi_ref, lo_ref):
    weight = tile[2] * (MASS_SHIFT + total)
    store_basis(tile, jnp.where(weight > 0.0, jnp.sqrt(weight), 0.0), hi_ref, lo_ref)


def mass_body(rows_ref, order, near, far, total_ref, mass_ref, flat, tile, hi, lo):
    parts = flat.shape[0] // near.shape[1]
    load_tile(order, near, far, rows_ref[pl.program_id(0)] * parts, flat, tile)
    store_mass(tile, total_ref[0], hi, lo)
    mass_ref[0] = nt(hi[...], hi[...]) + nt(lo[...], hi[...]) + nt(hi[...], lo[...])


def mass_windows(row_tiles, order, data, total):
    tile_rows = row_tiles.shape[0]
    flat_rows = TB // (M // (2 * data[0].shape[0])) * data[0].shape[1]
    return pl.pallas_call(
        mass_body,
        out_shape=jax.ShapeDtypeStruct((tile_rows, WIN, WIN), jnp.float32),
        grid_spec=pltpu.PrefetchScalarGridSpec(
            num_scalar_prefetch=2,
            grid=(tile_rows,),
            in_specs=[
                pl.BlockSpec(data[0].shape, lambda r, *_: (0, 0, 0)),
                pl.BlockSpec(data[0].shape, lambda r, *_: (0, 0, 0)),
                pl.BlockSpec((1, KROWS, TB), lambda r, *_: (r, 0, 0)),
            ],
            out_specs=pl.BlockSpec((1, WIN, WIN), lambda r, *_: (r, 0, 0)),
            scratch_shapes=[
                pltpu.VMEM((flat_rows, TB), jnp.float32),
                pltpu.VMEM((GROUPS, KROWS, TB), jnp.float32),
            ]
            + [pltpu.VMEM((WIN, POINTS), jnp.bfloat16)] * 2,
        ),
        compiler_params=pltpu.CompilerParams(vmem_limit_bytes=GRANT),
    )(row_tiles, order, *data, total)


def tiles_of_factor(conn, extract, points):
    count = conn.shape[0]
    grid_size = lax.axis_size("grid")
    blk_size = lax.axis_size("blk")
    grid_at = lax.axis_index("grid")
    blk_at = lax.axis_index("blk")
    tiles = M // TB
    tile_rows = tiles // grid_size
    tile_cols = tiles // blk_size

    own = local_pack(conn, extract, points, (blk_at * grid_size + grid_at) * count)
    data = gather_core(gather_blk(gather_z(own)))
    order = gathered_order()

    row_tiles = jnp.arange(tile_rows, dtype=jnp.int32) * grid_size + grid_at
    col_tiles = jnp.arange(tile_cols, dtype=jnp.int32) * blk_size + blk_at
    flat_at = blk_at * grid_size + grid_at
    total_devices = blk_size * grid_size
    unit = flat_at * count // UNIT
    start = (unit * UNIT - UNIT) % M
    firsts = jnp.stack([start // count % total_devices, (flat_at * count - start) % M])
    piece = panel_rows(count, firsts, order, data)
    share = piece
    if count < UNIT:
        share = lax.dynamic_slice_in_dim(piece, flat_at * count % UNIT, count, 0)
        share = jnp.concatenate([share, piece[UNIT:]], axis=0)
    stage = gather_z(share)
    after = lax.optimization_barrier((order, share))[0]
    parts = []
    for r in range(tile_rows):
        parts.append(stiffness_tiles(row_tiles[r : r + 1], col_tiles, after, data))
        if r == 0:
            stage, after = lax.optimization_barrier((stage, order))
    stage = gather_blk(stage)
    pieces = gather_core(stage)
    main = [part[0][0] for part in parts]
    pairs = [
        part[1].reshape(1, tile_cols // 2, 2, WIN, TB)[..., :HALO] for part in parts
    ]
    halo = jnp.concatenate(
        [jnp.concatenate([pair[:, :, 0], pair[:, :, 1]], axis=-1) for pair in pairs], axis=0
    )
    total = jnp.concatenate(lax.optimization_barrier([part[2] for part in parts]), axis=0)
    halo = jnp.concatenate([halo.reshape(-1, TB), total.reshape(-1, TB)], axis=0)
    halo = lax.ppermute(halo, "blk", ring(blk_size, 1))
    totals = [lax.ppermute(total, "blk", ring(blk_size, s)) for s in range(2, blk_size)]
    edge = tile_rows * tile_cols // 2 * WIN
    totals.append(halo[edge:].reshape(total.shape))
    total = functools.reduce(jnp.add, totals, total)
    head_mass, tail_mass = end_masses(count, order, data, pieces)
    mass = mass_windows(row_tiles, order, data, total)

    halo = halo[:edge].reshape(tile_rows, tile_cols // 2, WIN, TB)
    halo = jnp.stack([halo[..., :HALO], halo[..., HALO:]], axis=2)
    halo = halo.reshape(tile_rows, tile_cols, WIN, HALO)
    halo = jnp.where(blk_at == 0, jnp.roll(halo, 1, axis=1), halo)
    here = (col_tiles[None, :] == row_tiles[:, None])[:, :, None, None]
    after = (col_tiles[None, :] == (row_tiles[:, None] + 1) % tiles)[:, :, None, None]
    stiff = []
    for r in range(tile_rows):
        side = halo[r] + jnp.where(after[r], mass[r, None, :, TB:], 0.0)
        side = jnp.pad(side, ((0, 0), (0, 0), (0, TB - HALO)))
        stiff.append(main[r] + jnp.where(here[r], mass[r, None, :, :TB], 0.0) + side)

    below = jnp.stack([part[:, TB:, :] for part in stiff])
    below = lax.ppermute(below, "grid", ring(grid_size, 1))
    row_part, col_part = panel_factor(
        count, row_tiles, col_tiles, order, pieces, head_mass, tail_mass
    )
    below = jnp.where(grid_at == 0, jnp.roll(below, 1, axis=0), below)
    stiff = jnp.stack([part[:, :TB, :] for part in stiff]) + jnp.pad(
        below, ((0, 0), (0, 0), (0, TB - HALO), (0, 0))
    )
    update = jnp.einsum("xuw,yvw->xyuv", row_part, col_part, precision=lax.Precision.HIGHEST)
    tile_row = row_tiles[:, None, None, None]
    tile_col = col_tiles[None, :, None, None]
    whole_row = tile_row * TB + jnp.arange(TB, dtype=jnp.int32)[None, None, :, None]
    whole_col = tile_col * TB + jnp.arange(TB, dtype=jnp.int32)[None, None, None, :]
    result = jnp.where(
        tile_col == 0, row_part[:, None], jnp.where(tile_row == 0, 0.0, stiff - update)
    )
    return jnp.where(whole_row >= whole_col, result, 0.0).transpose(0, 2, 1, 3)


def solution(mesh):
    in_specs = (
        P(("blk", "grid"), None),
        P(None, None, ("blk", "grid")),
        P(None, None, ("blk", "grid")),
    )
    out_specs = P(None, "grid", None, "blk")
    return jax.shard_map(tiles_of_factor, mesh=mesh, in_specs=in_specs, out_specs=out_specs, check_vma=False)
```

```python
import functools
import math

import jax
import jax.numpy as jnp
from jax import lax
from jax.experimental import pallas as pl
from jax.experimental.pallas import tpu as pltpu
from jax.sharding import PartitionSpec as P


M = 2048
EX = 64
EY = 32
QP = 9
TB = 128

KERNEL_GAIN = 0.02
MASS_SHIFT = 0.05

TILE_IX = TB // EY
WIN_IX = TILE_IX + 2
WIN = WIN_IX * EY
HALO = WIN - TB
COLS = 256
POINTS = QP * TB
GROUPS = 3 + QP
KROWS = 16
GRANT = 24 << 20
UNIT = 2 * EY
EXTRA = (QP + 1) // 2
SIDE = POINTS // 2
STRIP = SIDE // 3
REACH = TILE_IX + 7
HALF = EX / 2.0
ROUND_X = 1.5 * 2.0**23 * HALF
ROUND_Y = 1.5 * 2.0**23 * (HALF * EY / EX)


def bernstein_table():
    spread_root = 0.5 * math.sqrt(0.6)
    gauss_nodes = [0.5 - spread_root, 0.5, 0.5 + spread_root]

    def bern_poly(which, where):
        return [(1.0 - where) ** 2, 2.0 * where * (1.0 - where), where * where][which]

    table_rows = []
    for i in range(3):
        for j in range(3):
            table_row = []
            for a in range(3):
                for b in range(3):
                    table_row.append(bern_poly(a, gauss_nodes[i]) * bern_poly(b, gauss_nodes[j]))
            table_rows.append(table_row)
    return jnp.asarray(table_rows, jnp.float32)


def ring(size, shift):
    return [(i, (i + shift) % size) for i in range(size)]


def gather_z(x):
    size = lax.axis_size("grid")
    return jnp.stack([x] + [lax.ppermute(x, "grid", ring(size, 2 * s)) for s in range(1, size // 2)])


def gather_blk(x):
    size = lax.axis_size("blk")
    return jnp.stack([x] + [lax.ppermute(x, "blk", ring(size, s)) for s in range(1, size)])


def gather_core(x):
    size = lax.axis_size("grid")
    x = x.reshape(-1, *x.shape[2:])
    return x, lax.ppermute(x, "grid", [(i, i ^ 1) for i in range(size)])


def fetch(near, far, place):
    depth = near.shape[0]
    return jnp.where(place < depth, near[place % depth], far[place % depth])


def gathered_order():
    grid_size, blk_size = lax.axis_size("grid"), lax.axis_size("blk")
    grid_at, blk_at = lax.axis_index("grid"), lax.axis_index("blk")
    depth = grid_size // 2
    flat = jnp.arange(blk_size * grid_size, dtype=jnp.int32)
    blk_of, grid_of = flat // grid_size, flat % grid_size
    core = grid_of % 2 ^ grid_at % 2
    return (core * blk_size + (blk_at - blk_of) % blk_size) * depth + (
        grid_at // 2 - grid_of // 2
    ) % depth


def local_pack(conn, extract, points, first):
    count = conn.shape[0]
    element = first + jnp.arange(count, dtype=jnp.int32)
    step_x = (conn // EY - (element // EY)[:, None]) % EX
    step_y = (conn % EY - (element % EY)[:, None]) % EY
    slot = (3 * step_x + step_y).T
    values = jnp.einsum("kb,abn->akn", bernstein_table(), extract, precision=lax.Precision.HIGHEST)
    names = jnp.arange(QP, dtype=jnp.int32)
    ordered = jnp.sum(
        jnp.where(slot[None, :, None, :] == names[:, None, None, None], values[None], 0.0), axis=1
    )
    kind = lax.broadcasted_iota(jnp.int32, points.shape, 0)
    scaled = points * jnp.where(kind < 2, HALF, 1.0)
    flat = jnp.concatenate([scaled, ordered], axis=0).reshape(GROUPS * QP, count)
    parts = TB // count
    height = -(-GROUPS * QP // parts // 8) * 8
    flat = jnp.pad(flat, ((0, parts * height - GROUPS * QP), (0, 0)))
    return flat.reshape(parts, height, count).transpose(1, 0, 2).reshape(height, TB)


def load_tile(order, near, far, first, flat, tile):
    total, height = 2 * near.shape[0], near.shape[1]
    parts = flat.shape[0] // height
    count = TB // parts
    segment = lax.broadcasted_iota(jnp.int32, (height, TB), 1) // count
    pieces = [fetch(near, far, order[(first + i) % total]) for i in range(parts)]
    for m in range(parts):
        rows = jnp.zeros((height, TB), jnp.float32)
        for i in range(parts):
            shift = (i - m) * count % TB
            turned = pltpu.roll(pieces[i], shift, 1) if shift else pieces[i]
            rows = jnp.where(segment == i, turned, rows)
        flat[m * height : (m + 1) * height] = rows
    tile[:, QP:, :] = jnp.zeros((GROUPS, KROWS - QP, TB), jnp.float32)
    for group in range(GROUPS):
        tile[group, :QP, :] = flat[group * QP : (group + 1) * QP, :]


def store_basis(tile, scale, hi_ref, lo_ref, columns=range(WIN_IX)):
    lane = lax.broadcasted_iota(jnp.int32, (1, TB), 1)
    column = lane // EY
    fy = lax.broadcasted_iota(jnp.int32, (EY, TB), 0)
    iy = lax.broadcasted_iota(jnp.int32, (EY, TB), 1) % EY
    step = (fy - iy + EY) % EY
    masks = [step == t for t in range(3)]
    for place, fx in enumerate(columns):
        hi, lo = [], []
        for t in range(3):
            rows = jnp.zeros((KROWS, TB), jnp.float32)
            for ix in range(TILE_IX):
                if 0 <= fx - ix < 3:
                    rows = jnp.where(column == ix, tile[3 + 3 * (fx - ix) + t], rows)
            rows = rows * scale
            top = rows.astype(jnp.bfloat16).astype(jnp.float32)
            hi.append(top)
            lo.append(rows - top)
        for k in range(QP):
            for parts, ref in ((hi, hi_ref), (lo, lo_ref)):
                block = jnp.zeros((EY, TB), jnp.float32)
                for t in range(3):
                    block = jnp.where(masks[t], parts[t][k : k + 1], block)
                ref[place * EY : (place + 1) * EY, k * TB : (k + 1) * TB] = block.astype(jnp.bfloat16)


def store_weight(tile, hi_ref, lo_ref):
    first = lax.broadcasted_iota(jnp.int32, (COLS - WIN, TB), 0) == 0
    rows = tile[2]
    top = rows.astype(jnp.bfloat16).astype(jnp.float32)
    for k in range(QP):
        for part, ref in ((top, hi_ref), (rows - top, lo_ref)):
            block = jnp.where(first, part[k : k + 1], 0.0)
            ref[WIN:, k * TB : (k + 1) * TB] = block.astype(jnp.bfloat16)


def nt(a, b):
    return lax.dot_general(a, b, (((1,), (1,)), ((), ())), preferred_element_type=jnp.float32)


def nn(a, b):
    return lax.dot_general(a, b, (((1,), (0,)), ((), ())), preferred_element_type=jnp.float32)


def kernel_block(xp, yp, xq, yq, wrapped):
    gx = xp - xq
    if wrapped:
        gx = gx - ((gx + ROUND_X) - ROUND_X)
    gy = yp - yq
    gy = gy - ((gy + ROUND_Y) - ROUND_Y)
    return jnp.exp2(-1.75 * jnp.log2(gx * gx + gy * gy + 1.0))


def store_columns(row, ref, at):
    ref[at : at + TB, :] = jnp.broadcast_to(row, (TB, TB)).T


def tile_body(
    tile_cols, last, rows_ref, cols_ref, order, near, far, main_ref, halo_ref, total_ref,
    flat, rtile, ctile, xp_ref, yp_ref, rhi, rlo, chi, clo, gtop, gend, pot, ytop, yrest, qx,
):
    t = pl.program_id(0)
    c = t % tile_cols
    before = (t + tile_cols - 1) % tile_cols
    parts = flat.shape[0] // near.shape[1]
    busy = t < last
    step_rows = 32
    tiles = M // TB
    offset = rows_ref[jnp.minimum(t, last - 1) // tile_cols] - cols_ref[c]
    apart = jnp.abs(offset)
    unsure = jnp.logical_and(
        TILE_IX * apart + REACH > EX // 2, TILE_IX * (tiles - apart) + REACH > EX // 2
    )

    def contract(at, g_ref, i):
        rows = pl.ds(pl.multiple_of(i * STRIP, STRIP), STRIP)
        g = g_ref[rows, :]
        pot[pl.ds(pl.multiple_of(at + i * STRIP, STRIP), STRIP), :] = nt(g, chi[...]) + nt(g, clo[...])

    def sweep(at, g_ref, other, other_ref, wrapped):
        @pl.loop(0, SIDE // STRIP)
        def _(i):
            for j in range(STRIP // step_rows):
                rows = pl.ds(pl.multiple_of(at + i * STRIP + j * step_rows, step_rows), step_rows)
                into = pl.ds(pl.multiple_of(i * STRIP + j * step_rows, step_rows), step_rows)
                xp, yp = xp_ref[rows, :], yp_ref[rows, :]
                for k in range(QP):
                    g = kernel_block(xp, yp, qx[k : k + 1, :], ctile[1, k : k + 1, :], wrapped)
                    g_ref[into, k * TB : (k + 1) * TB] = g.astype(jnp.bfloat16)
            contract(other, other_ref, i)

    def split():
        for k in range(QP):
            turned = pot[k * TB : (k + 1) * TB, TB:].T
            old = jnp.where(before == 0, 0.0, total_ref[0, k : k + 1, :])
            total_ref[0, k : k + 1, :] = old + KERNEL_GAIN * turned[HALO : HALO + 1, :]
        total_ref[0, QP:, :] = jnp.zeros((KROWS - QP, TB), jnp.float32)
        for k in range(QP):
            rows = slice(k * TB, (k + 1) * TB)
            full = pot[rows, :]
            top = full.astype(jnp.bfloat16)
            ytop[rows, :] = top
            yrest[rows, :] = (full - top.astype(jnp.float32)).astype(jnp.bfloat16)

    def finish():
        stiff = nn(rhi[...], ytop[...]) + nn(rlo[...], ytop[...]) + nn(rhi[...], yrest[...])
        main_ref[0, 0] = -KERNEL_GAIN * stiff[:, :TB]
        halo_ref[0, 0] = -KERNEL_GAIN * stiff[:, TB:]

    @pl.when(jnp.logical_and(busy, c == 0))
    def _():
        load_tile(order, near, far, rows_ref[t // tile_cols] * parts, flat, rtile)
        for k in range(QP):
            store_columns(rtile[0, k : k + 1, :], xp_ref, k * TB)
            store_columns(rtile[1, k : k + 1, :], yp_ref, k * TB)

    @pl.when(busy)
    def _():
        load_tile(order, near, far, cols_ref[c] * parts, flat, ctile)
        image = jnp.where(unsure, 0, (2 * offset > tiles).astype(jnp.int32) - (2 * offset < -tiles).astype(jnp.int32))
        qx[...] = ctile[0] + image.astype(jnp.float32) * HALF

    for wrapped in (False, True):

        @pl.when(jnp.logical_and(busy, unsure == wrapped))
        def _(wrapped=wrapped):
            sweep(0, gtop, SIDE, gend, wrapped)

    @pl.when(busy)
    def _():
        split()
        finish()
        store_basis(ctile, ctile[2], chi, clo)
        store_weight(ctile, chi, clo)

    for wrapped in (False, True):

        @pl.when(jnp.logical_and(busy, unsure == wrapped))
        def _(wrapped=wrapped):
            sweep(SIDE, gend, 0, gtop, wrapped)

    @pl.when(jnp.logical_and(busy, c == 0))
    def _():
        store_basis(rtile, rtile[2], rhi, rlo)

    @pl.when(t == last)
    def _():
        @pl.loop(0, SIDE // STRIP)
        def _(i):
            contract(SIDE, gend, i)

        split()
        finish()


def stiffness_tiles(row_tiles, col_tiles, order, data):
    tile_rows, tile_cols = row_tiles.shape[0], col_tiles.shape[0]
    count = M // (2 * data[0].shape[0])
    flat_rows = TB // count * data[0].shape[1]
    last = tile_rows * tile_cols
    f32, b16 = jnp.float32, jnp.bfloat16

    def done(t):
        return jnp.maximum(t - 1, 0)

    return pl.pallas_call(
        functools.partial(tile_body, tile_cols, last),
        out_shape=(
            jax.ShapeDtypeStruct((tile_rows, tile_cols, WIN, TB), f32),
            jax.ShapeDtypeStruct((tile_rows, tile_cols, WIN, TB), f32),
            jax.ShapeDtypeStruct((tile_rows, KROWS, TB), f32),
        ),
        grid_spec=pltpu.PrefetchScalarGridSpec(
            num_scalar_prefetch=3,
            grid=(last + 1,),
            in_specs=[pl.BlockSpec(data[0].shape, lambda t, *_: (0, 0, 0))] * 2,
            out_specs=(
                pl.BlockSpec((1, 1, WIN, TB), lambda t, *_: (done(t) // tile_cols, done(t) % tile_cols, 0, 0)),
                pl.BlockSpec((1, 1, WIN, TB), lambda t, *_: (done(t) // tile_cols, done(t) % tile_cols, 0, 0)),
                pl.BlockSpec((1, KROWS, TB), lambda t, *_: (done(t) // tile_cols, 0, 0)),
            ),
            scratch_shapes=[
                pltpu.VMEM((flat_rows, TB), f32),
                pltpu.VMEM((GROUPS, KROWS, TB), f32),
                pltpu.VMEM((GROUPS, KROWS, TB), f32),
                pltpu.VMEM((POINTS, TB), f32),
                pltpu.VMEM((POINTS, TB), f32),
                pltpu.VMEM((WIN, POINTS), b16),
                pltpu.VMEM((WIN, POINTS), b16),
                pltpu.VMEM((COLS, POINTS), b16),
                pltpu.VMEM((COLS, POINTS), b16),
                pltpu.VMEM((SIDE, POINTS), b16),
                pltpu.VMEM((SIDE, POINTS), b16),
                pltpu.VMEM((POINTS, COLS), f32),
                pltpu.VMEM((POINTS, COLS), b16),
                pltpu.VMEM((POINTS, COLS), b16),
                pltpu.VMEM((KROWS, TB), f32),
            ],
        ),
        compiler_params=pltpu.CompilerParams(vmem_limit_bytes=GRANT),
        cost_estimate=pl.CostEstimate(
            flops=last * 2 * 10**9, bytes_accessed=2 * 10**6, transcendentals=last * 2 * POINTS**2
        ),
    )(row_tiles, col_tiles, order, *data)


def pack_half(rows):
    low = lax.broadcasted_iota(jnp.int32, (1, TB), 1) < TB // 2
    turned = pltpu.roll(rows, TB // 2, 1)
    return [
        jnp.where(low, turned[2 * m : 2 * m + 1], rows[2 * m + 1 : 2 * m + 2]) for m in range(EXTRA)
    ]


def panel_body(
    count, firsts, order, near, far, out_ref, flat, ptile, htile, ttile, xp_ref, yp_ref, phi, plain_hi, plain_lo,
    side_hi, side_lo, qx, qy, weights, gtop, gend, pot, sums, halves,
):
    parts = flat.shape[0] // near.shape[1]
    total = 2 * near.shape[0]
    load_tile(order, near, far, firsts[0], flat, ptile)
    load_tile(order, near, far, 0, flat, htile)
    load_tile(order, near, far, total - parts, flat, ttile)
    lane = lax.broadcasted_iota(jnp.int32, (1, TB), 1)
    own = jnp.logical_and(lane >= firsts[1], lane < firsts[1] + count)
    weight = jnp.where(own, ptile[2], 0.0)
    top = weight.astype(jnp.bfloat16).astype(jnp.float32)
    for k in range(QP):
        store_columns(ptile[0, k : k + 1, :], xp_ref, k * TB)
        store_columns(ptile[1, k : k + 1, :], yp_ref, k * TB)
        first = lax.broadcasted_iota(jnp.int32, (KROWS, TB), 0)
        both = jnp.where(
            first == 0, top[k : k + 1], jnp.where(first == 1, (weight - top)[k : k + 1], 0.0)
        )
        weights[k] = both.astype(jnp.bfloat16)
    for group, ref in ((0, qx), (1, qy)):
        ref[:QP, :] = htile[group, :QP, :]
        for m, row in enumerate(pack_half(ttile[group])):
            ref[QP + m : QP + m + 1, :] = row
    store_basis(htile, htile[2], plain_hi, plain_lo, range(TILE_IX))
    phi[:TB, :POINTS] = plain_hi[...]
    phi[TB:, :POINTS] = plain_lo[...]
    fy = lax.broadcasted_iota(jnp.int32, (EY, TB), 0)
    iy = lax.broadcasted_iota(jnp.int32, (EY, TB), 1) % EY
    step = (fy - iy + EY) % EY
    column = lane // EY
    phi[:, POINTS:] = jnp.zeros((2 * TB, EXTRA * TB), jnp.bfloat16)
    for place in range(WIN_IX - TILE_IX):
        fx = TILE_IX + place
        packs = []
        for t in range(3):
            rows = jnp.zeros((KROWS, TB), jnp.float32)
            for ix in range(TILE_IX):
                if 0 <= fx - ix < 3:
                    rows = jnp.where(column == ix, ttile[3 + 3 * (fx - ix) + t], rows)
            packs.append(pack_half(rows * ttile[2]))
        for m in range(EXTRA):
            block = jnp.zeros((EY, TB), jnp.float32)
            for t in range(3):
                block = jnp.where(step == t, packs[t][m], block)
            upper = block.astype(jnp.bfloat16)
            lanes = slice(POINTS + m * TB, POINTS + (m + 1) * TB)
            phi[place * EY : (place + 1) * EY, lanes] = upper
            phi[TB + place * EY : TB + (place + 1) * EY, lanes] = (
                block - upper.astype(jnp.float32)
            ).astype(jnp.bfloat16)
    store_basis(ptile, ptile[2], side_hi, side_lo, (2, 3))
    sums[...] = jnp.zeros_like(sums)
    step_rows = 32

    def evaluate(strip, g_ref):
        for j in range(TB // step_rows):
            rows = pl.ds(pl.multiple_of(strip * TB + j * step_rows, step_rows), step_rows)
            xp, yp = xp_ref[rows, :], yp_ref[rows, :]
            for k in range(QP + EXTRA):
                g = kernel_block(xp, yp, qx[k : k + 1, :], qy[k : k + 1, :], True)
                g_ref[j * step_rows : (j + 1) * step_rows, k * TB : (k + 1) * TB] = g.astype(
                    jnp.bfloat16
                )

    def contract(strip, g_ref, valid):
        g = g_ref[...]
        pot[pl.ds(pl.multiple_of(strip * TB, TB), TB), :] = nt(g, phi[...])
        sums[...] += jnp.where(valid, nn(weights[strip], g), 0.0)

    @pl.loop(0, QP // 2)
    def _(i):
        evaluate(2 * i, gtop)
        contract(jnp.maximum(2 * i - 1, 0), gend, i > 0)
        evaluate(2 * i + 1, gend)
        contract(2 * i, gtop, True)

    evaluate(QP - 1, gtop)
    contract(QP - 2, gend, True)
    contract(QP - 1, gtop, True)
    for k in range(QP):
        rows = slice(k * TB, (k + 1) * TB)
        full = pot[rows, :TB] + pot[rows, TB:]
        upper = full.astype(jnp.bfloat16)
        halves[rows, :TB] = upper
        halves[rows, TB:] = (full - upper.astype(jnp.float32)).astype(jnp.bfloat16)
    wide = nn(side_hi[...], halves[...])
    panel = wide[:, :TB] + wide[:, TB:] + nn(side_lo[...], halves[:, :TB])
    out_ref[:UNIT, :] = -KERNEL_GAIN * panel
    out_ref[UNIT:, :] = jnp.zeros((KROWS, TB), jnp.float32)
    for m in range(QP + EXTRA):
        lanes = slice(m * TB, (m + 1) * TB)
        out_ref[UNIT + m : UNIT + m + 1, :] = KERNEL_GAIN * (sums[0:1, lanes] + sums[1:2, lanes])


def panel_rows(count, firsts, order, data):
    flat_rows = TB // count * data[0].shape[1]
    f32, b16 = jnp.float32, jnp.bfloat16
    tile = pltpu.VMEM((GROUPS, KROWS, TB), f32)
    width = (QP + EXTRA) * TB
    return pl.pallas_call(
        functools.partial(panel_body, count),
        out_shape=jax.ShapeDtypeStruct((UNIT + KROWS, TB), f32),
        grid_spec=pltpu.PrefetchScalarGridSpec(
            num_scalar_prefetch=2,
            grid=(1,),
            in_specs=[pl.BlockSpec(data[0].shape, lambda i, *_: (0, 0, 0))] * 2,
            out_specs=pl.BlockSpec((UNIT + KROWS, TB), lambda i, *_: (0, 0)),
            scratch_shapes=[
                pltpu.VMEM((flat_rows, TB), f32), tile, tile, tile,
                pltpu.VMEM((POINTS, TB), f32), pltpu.VMEM((POINTS, TB), f32),
                pltpu.VMEM((2 * TB, width), b16),
                pltpu.VMEM((TB, POINTS), b16), pltpu.VMEM((TB, POINTS), b16),
                pltpu.VMEM((UNIT, POINTS), b16), pltpu.VMEM((UNIT, POINTS), b16),
                pltpu.VMEM((KROWS, TB), f32), pltpu.VMEM((KROWS, TB), f32),
                pltpu.VMEM((QP, KROWS, TB), b16),
                pltpu.VMEM((TB, width), b16), pltpu.VMEM((TB, width), b16),
                pltpu.VMEM((POINTS, 2 * TB), f32),
                pltpu.VMEM((KROWS, width), f32),
                pltpu.VMEM((POINTS, 2 * TB), b16),
            ],
        ),
        compiler_params=pltpu.CompilerParams(vmem_limit_bytes=GRANT),
        cost_estimate=pl.CostEstimate(flops=2 * 10**9, bytes_accessed=10**6, transcendentals=4 * 10**6),
    )(firsts, order, *data)


def halves_of(a):
    top = a.astype(jnp.bfloat16)
    return top, (a - top.astype(jnp.float32)).astype(jnp.bfloat16)


def cholesky_and_inverse(head):
    step = 8
    blocks = TB // step
    lane = lax.broadcasted_iota(jnp.int32, (step, TB), 1)
    sub = lax.broadcasted_iota(jnp.int32, (step, TB), 0)
    left = [head[i * step : (i + 1) * step] for i in range(blocks)]
    right = [(lane == sub + i * step).astype(jnp.float32) for i in range(blocks)]
    roots = []
    for at in range(blocks):
        later = range(at, blocks)
        column = [
            {i: jnp.broadcast_to(left[i][:, at * step + j : at * step + j + 1], (step, TB)) for i in later}
            for j in range(step)
        ]
        for row in range(step):
            pivot = jnp.broadcast_to(column[row][at][row : row + 1], (step, TB))
            scale = 1.0 / pivot
            roots.append(pivot)
            left_row = jnp.broadcast_to(left[at][row : row + 1], (step, TB)) * scale
            right_row = jnp.broadcast_to(right[at][row : row + 1], (step, TB)) * scale
            ahead = {
                j: jnp.broadcast_to(column[j][at][row : row + 1], (step, TB)) * scale
                for j in range(row + 1, step)
            }
            for i in later:
                factor = column[row][i]
                if i == at:
                    factor = jnp.where(sub > row, factor, 0.0)
                for j in range(row + 1, step):
                    column[j][i] = column[j][i] - factor * ahead[j]
                left[i] = left[i] - factor * left_row
                right[i] = right[i] - factor * right_row
    uppers, inverses = [], []
    for i in range(blocks):
        pivots = roots[i * step]
        for row in range(1, step):
            pivots = jnp.where(sub == row, roots[i * step + row], pivots)
        root = lax.rsqrt(pivots)
        uppers.append(jnp.where(lane >= sub + i * step, left[i] * root, 0.0))
        inverses.append(right[i] * root)
    return jnp.concatenate(uppers, axis=0).T, jnp.concatenate(inverses, axis=0)


def ends_body(count, order, near, far, pieces_near, pieces_far, head_mass, tail_mass, flat, tile, hi, lo):
    parts = TB // count
    total = 2 * near.shape[0]
    sums = jnp.zeros((KROWS, TB), jnp.float32)
    for d in range(total // 2):
        sums = sums + (pieces_near[d, count:, :] + pieces_far[d, count:, :])
    lane = lax.broadcasted_iota(jnp.int32, (1, TB), 1)
    turned = pltpu.roll(sums, TB // 2, 1)
    last = jnp.concatenate(
        [(turned, sums)[k % 2][QP + k // 2 : QP + k // 2 + 1] for k in range(QP)]
        + [jnp.zeros((KROWS - QP, TB), jnp.float32)],
        axis=0,
    )
    last = jnp.where(lane >= TB // 2, last, 0.0)
    for first, value, ref, cols in (
        (0, sums, head_mass, slice(0, TB)),
        (total - parts, last, tail_mass, slice(TB, WIN)),
    ):
        load_tile(order, near, far, first, flat, tile)
        store_mass(tile, value, hi, lo)
        ref[:, : cols.stop - cols.start] = (
            nt(hi[...], hi[cols, :]) + nt(lo[...], hi[cols, :]) + nt(hi[...], lo[cols, :])
        )


def end_masses(count, order, data, pieces):
    flat_rows = TB // count * data[0].shape[1]
    f32, b16 = jnp.float32, jnp.bfloat16
    basis = pltpu.VMEM((WIN, POINTS), b16)
    return pl.pallas_call(
        functools.partial(ends_body, count),
        out_shape=(jax.ShapeDtypeStruct((WIN, TB), f32), jax.ShapeDtypeStruct((WIN, TB), f32)),
        grid_spec=pltpu.PrefetchScalarGridSpec(
            num_scalar_prefetch=1,
            grid=(1,),
            in_specs=[
                pl.BlockSpec(data[0].shape, lambda i, *_: (0, 0, 0)),
                pl.BlockSpec(data[0].shape, lambda i, *_: (0, 0, 0)),
                pl.BlockSpec(pieces[0].shape, lambda i, *_: (0, 0, 0)),
                pl.BlockSpec(pieces[0].shape, lambda i, *_: (0, 0, 0)),
            ],
            out_specs=(
                pl.BlockSpec((WIN, TB), lambda i, *_: (0, 0)),
                pl.BlockSpec((WIN, TB), lambda i, *_: (0, 0)),
            ),
            scratch_shapes=[
                pltpu.VMEM((flat_rows, TB), f32), pltpu.VMEM((GROUPS, KROWS, TB), f32),
                basis, basis,
            ],
        ),
        compiler_params=pltpu.CompilerParams(vmem_limit_bytes=GRANT),
        cost_estimate=pl.CostEstimate(flops=2 * 10**9, bytes_accessed=2 * 10**6, transcendentals=0),
    )(order, *data, *pieces)


def factor_body(
    count, rows_ref, cols_ref, order, near, far, head_mass, tail_mass, rowp_ref, colp_ref, low, inverse
):
    parts = TB // count
    tiles = M // TB

    def panel_tile(index):
        rows = jnp.concatenate(
            [fetch(near, far, order[index * parts + i])[:count, :] for i in range(parts)], axis=0
        )
        side = jnp.zeros((TB, TB - HALO), jnp.float32)
        below = jnp.zeros((TB - HALO, TB), jnp.float32)
        tail = tail_mass[:, :HALO]
        corner = jnp.concatenate([tail[TB:], jnp.zeros((TB - HALO, HALO), jnp.float32)], axis=0)
        here = head_mass[:TB] + jnp.concatenate([corner, side], axis=1)
        after = jnp.concatenate([head_mass[TB:], below], axis=0)
        before = jnp.concatenate([tail[:TB], side], axis=1)
        rows = rows + jnp.where(index == 0, here, 0.0) + jnp.where(index == 1, after, 0.0)
        return rows + jnp.where(index == tiles - 1, before, 0.0)

    head = panel_tile(0)
    lower, inv = cholesky_and_inverse(0.5 * (head + head.T))
    low[...] = lower
    inverse[...] = inv
    inv_hi, inv_lo = halves_of(inverse[...])
    for ref, indices in ((rowp_ref, rows_ref), (colp_ref, cols_ref)):
        for i in range(ref.shape[0]):
            top, rest = halves_of(panel_tile(indices[i]))
            solved = nt(top, inv_hi) + nt(top, inv_lo) + nt(rest, inv_hi)
            ref[i] = jnp.where(indices[i] == 0, low[...], solved)


def panel_factor(count, row_tiles, col_tiles, order, pieces, head_mass, tail_mass):
    tile_rows, tile_cols = row_tiles.shape[0], col_tiles.shape[0]
    f32 = jnp.float32
    return pl.pallas_call(
        functools.partial(factor_body, count),
        out_shape=(
            jax.ShapeDtypeStruct((tile_rows, TB, TB), f32),
            jax.ShapeDtypeStruct((tile_cols, TB, TB), f32),
        ),
        grid_spec=pltpu.PrefetchScalarGridSpec(
            num_scalar_prefetch=3,
            grid=(1,),
            in_specs=[
                pl.BlockSpec(pieces[0].shape, lambda i, *_: (0, 0, 0)),
                pl.BlockSpec(pieces[0].shape, lambda i, *_: (0, 0, 0)),
                pl.BlockSpec((WIN, TB), lambda i, *_: (0, 0)),
                pl.BlockSpec((WIN, TB), lambda i, *_: (0, 0)),
            ],
            out_specs=(
                pl.BlockSpec((tile_rows, TB, TB), lambda i, *_: (0, 0, 0)),
                pl.BlockSpec((tile_cols, TB, TB), lambda i, *_: (0, 0, 0)),
            ),
            scratch_shapes=[pltpu.VMEM((TB, TB), f32), pltpu.VMEM((TB, TB), f32)],
        ),
        compiler_params=pltpu.CompilerParams(vmem_limit_bytes=GRANT),
        cost_estimate=pl.CostEstimate(flops=4 * 10**9, bytes_accessed=2 * 10**6, transcendentals=0),
    )(row_tiles, col_tiles, order, *pieces, head_mass, tail_mass)


def store_mass(tile, total, hi_ref, lo_ref):
    weight = tile[2] * (MASS_SHIFT + total)
    store_basis(tile, jnp.where(weight > 0.0, jnp.sqrt(weight), 0.0), hi_ref, lo_ref)


def mass_body(rows_ref, order, near, far, total_ref, mass_ref, flat, tile, hi, lo):
    parts = flat.shape[0] // near.shape[1]
    load_tile(order, near, far, rows_ref[pl.program_id(0)] * parts, flat, tile)
    store_mass(tile, total_ref[0], hi, lo)
    mass_ref[0] = nt(hi[...], hi[...]) + nt(lo[...], hi[...]) + nt(hi[...], lo[...])


def mass_windows(row_tiles, order, data, total):
    tile_rows = row_tiles.shape[0]
    flat_rows = TB // (M // (2 * data[0].shape[0])) * data[0].shape[1]
    return pl.pallas_call(
        mass_body,
        out_shape=jax.ShapeDtypeStruct((tile_rows, WIN, WIN), jnp.float32),
        grid_spec=pltpu.PrefetchScalarGridSpec(
            num_scalar_prefetch=2,
            grid=(tile_rows,),
            in_specs=[
                pl.BlockSpec(data[0].shape, lambda r, *_: (0, 0, 0)),
                pl.BlockSpec(data[0].shape, lambda r, *_: (0, 0, 0)),
                pl.BlockSpec((1, KROWS, TB), lambda r, *_: (r, 0, 0)),
            ],
            out_specs=pl.BlockSpec((1, WIN, WIN), lambda r, *_: (r, 0, 0)),
            scratch_shapes=[
                pltpu.VMEM((flat_rows, TB), jnp.float32),
                pltpu.VMEM((GROUPS, KROWS, TB), jnp.float32),
            ]
            + [pltpu.VMEM((WIN, POINTS), jnp.bfloat16)] * 2,
        ),
        compiler_params=pltpu.CompilerParams(vmem_limit_bytes=GRANT),
    )(row_tiles, order, *data, total)


def tiles_of_factor(conn, extract, points):
    count = conn.shape[0]
    grid_size = lax.axis_size("grid")
    blk_size = lax.axis_size("blk")
    grid_at = lax.axis_index("grid")
    blk_at = lax.axis_index("blk")
    tiles = M // TB
    tile_rows = tiles // grid_size
    tile_cols = tiles // blk_size

    own = local_pack(conn, extract, points, (blk_at * grid_size + grid_at) * count)
    data = gather_core(gather_blk(gather_z(own)))
    order = gathered_order()

    row_tiles = jnp.arange(tile_rows, dtype=jnp.int32) * grid_size + grid_at
    col_tiles = jnp.arange(tile_cols, dtype=jnp.int32) * blk_size + blk_at
    flat_at = blk_at * grid_size + grid_at
    total_devices = blk_size * grid_size
    unit = flat_at * count // UNIT
    start = (unit * UNIT - UNIT) % M
    firsts = jnp.stack([start // count % total_devices, (flat_at * count - start) % M])
    piece = panel_rows(count, firsts, order, data)
    share = piece
    if count < UNIT:
        share = lax.dynamic_slice_in_dim(piece, flat_at * count % UNIT, count, 0)
        share = jnp.concatenate([share, piece[UNIT:]], axis=0)
    stage = gather_z(share)
    after = lax.optimization_barrier((order, share))[0]
    parts = []
    for r in range(tile_rows):
        parts.append(stiffness_tiles(row_tiles[r : r + 1], col_tiles, after, data))
        if r == 0:
            stage, after = lax.optimization_barrier((stage, order))
    stage = gather_blk(stage)
    pieces = gather_core(stage)
    main = [part[0][0] for part in parts]
    halos = []
    for part in parts:
        pair = part[1].reshape(1, tile_cols // 2, 2, WIN, TB)[..., :HALO]
        halos.append(jnp.concatenate([pair[:, :, 0], pair[:, :, 1]], axis=-1))
    total = jnp.concatenate(lax.optimization_barrier([part[2] for part in parts]), axis=0)
    early = [lax.ppermute(halo, "blk", ring(blk_size, 1)) for halo in halos[:-1]]
    late = jnp.concatenate([halos[-1].reshape(-1, TB), total.reshape(-1, TB)], axis=0)
    late = lax.ppermute(late, "blk", ring(blk_size, 1))
    totals = [lax.ppermute(total, "blk", ring(blk_size, s)) for s in range(2, blk_size)]
    edge = tile_cols // 2 * WIN
    totals.append(late[edge:].reshape(total.shape))
    total = functools.reduce(jnp.add, totals, total)
    head_mass, tail_mass = end_masses(count, order, data, pieces)
    mass = mass_windows(row_tiles, order, data, total)

    halo = jnp.concatenate([*early, late[:edge].reshape(halos[-1].shape)], axis=0)
    halo = jnp.stack([halo[..., :HALO], halo[..., HALO:]], axis=2)
    halo = halo.reshape(tile_rows, tile_cols, WIN, HALO)
    halo = jnp.where(blk_at == 0, jnp.roll(halo, 1, axis=1), halo)
    here = (col_tiles[None, :] == row_tiles[:, None])[:, :, None, None]
    after = (col_tiles[None, :] == (row_tiles[:, None] + 1) % tiles)[:, :, None, None]
    stiff = []
    for r in range(tile_rows):
        side = halo[r] + jnp.where(after[r], mass[r, None, :, TB:], 0.0)
        side = jnp.pad(side, ((0, 0), (0, 0), (0, TB - HALO)))
        stiff.append(main[r] + jnp.where(here[r], mass[r, None, :, :TB], 0.0) + side)

    below = jnp.stack([part[:, TB:, :] for part in stiff])
    below = lax.ppermute(below, "grid", ring(grid_size, 1))
    row_part, col_part = panel_factor(
        count, row_tiles, col_tiles, order, pieces, head_mass, tail_mass
    )
    below = jnp.where(grid_at == 0, jnp.roll(below, 1, axis=0), below)
    stiff = jnp.stack([part[:, :TB, :] for part in stiff]) + jnp.pad(
        below, ((0, 0), (0, 0), (0, TB - HALO), (0, 0))
    )
    update = jnp.einsum("xuw,yvw->xyuv", row_part, col_part, precision=lax.Precision.HIGHEST)
    tile_row = row_tiles[:, None, None, None]
    tile_col = col_tiles[None, :, None, None]
    whole_row = tile_row * TB + jnp.arange(TB, dtype=jnp.int32)[None, None, :, None]
    whole_col = tile_col * TB + jnp.arange(TB, dtype=jnp.int32)[None, None, None, :]
    result = jnp.where(
        tile_col == 0, row_part[:, None], jnp.where(tile_row == 0, 0.0, stiff - update)
    )
    return jnp.where(whole_row >= whole_col, result, 0.0).transpose(0, 2, 1, 3)


def solution(mesh):
    in_specs = (
        P(("blk", "grid"), None),
        P(None, None, ("blk", "grid")),
        P(None, None, ("blk", "grid")),
    )
    out_specs = P(None, "grid", None, "blk")
    return jax.shard_map(tiles_of_factor, mesh=mesh, in_specs=in_specs, out_specs=out_specs, check_vma=False)
```
